32 devices in a mesh: tm: 8 (over z, core), lat: 4 (over y, x).
Axes of the slice: x: 2, y: 2, z: 4, core: 2. Of those that a mesh axis runs over, the one named last changes fastest.
Arguments:
- states: float32 [4, 8, 128, 2048], P(None, 'tm', 'lat'), may hold values from -6 to 6
- mass_term: float32 [128, 2048], P('lat'), may hold values from 0.005 to 0.05
- lat_coupling: float32 [128, 2048], P('lat'), may hold values from 0.25 to 2
- lon_coupling: float32 [128, 2048], P('lat'), may hold values from 0.25 to 2
Outputs:
- result: float32 [4, 8, 128, 2048], P(None, 'tm', 'lat')
The draws below stay inside these ranges and needn't reach their ends.
All inputs are finite; a program needn't handle non-finite values.
Results may differ from the reference program's by a relative error of at most 0.0003.
Values sent between devices are 32-bit elements; how exact they have to be, the bound alone decides.
No kernel may reach another device: no remote copies, remote signals or barrier semaphores. Data moves between devices by JAX's collectives and lax.ppermute only.
A program may use at most 64 MiB of HBM per device.

```python
import math
import jax
import jax.numpy as jnp
from jax import lax

FIELDS = 4
NLON = 2048
SWEEPS = 16
NLAT = 128
SUBWIN = 8


def draw_states(key, part):
    full_shape = (FIELDS, SUBWIN, NLAT, NLON)
    values = jnp.clip(jax.random.normal(key, full_shape, jnp.float32), -6.0, 6.0)
    return values


def steps_of(stream_key, shape, split, smallest, top_value):
    loudness = 1.0
    for dim, blocks in split:
        draws = jax.random.uniform(jax.random.fold_in(jax.random.fold_in(stream_key, 6), dim), (blocks,), jnp.float32, smallest / len(split), top_value / len(split))
        loudness = loudness * jnp.repeat(jnp.exp(draws), shape[dim] // blocks).reshape((-1,) + (1,) * (len(shape) - 1 - dim))
    return loudness


def setup_inputs(seed: int = 0) -> dict:
    key_list = jax.random.split(jax.random.key(seed), 5)
    return {
        "states": draw_states(jax.random.fold_in(key_list[4], 71), 0),
        "mass_term": jnp.clip(0.005 + 0.045 * jax.random.uniform(key_list[1], (NLAT, NLON), jnp.float32) ** steps_of(key_list[1], (NLAT, NLON), ((0, 4),), -0.2, 0.2), 0.005, 0.05),
        "lat_coupling": jnp.clip(jnp.exp(math.log(2.0) - 2.0794415 * jax.random.uniform(key_list[2], (NLAT, NLON), jnp.float32) ** steps_of(key_list[2], (NLAT, NLON), ((0, 4),), -0.2, 0.2)), 0.25, 2.0),
        "lon_coupling": jnp.clip(jnp.exp(math.log(2.0) - 2.0794415 * jax.random.uniform(key_list[3], (NLAT, NLON), jnp.float32) ** steps_of(key_list[3], (NLAT, NLON), ((0, 4),), -0.2, 0.2)), 0.25, 2.0),
    }


mass_low = 0.005
mass_high = 0.05
coupling_high = 2.0
base_shift = 0.002
time_coupling = 0.05

def time_basis(total_times):
    time_steps = jnp.arange(total_times, dtype=jnp.float32)
    freq_index = jnp.arange(total_times, dtype=jnp.int32)
    half_count = total_times // 2
    frequency = jnp.where(freq_index <= half_count, freq_index, freq_index - half_count).astype(jnp.float32)
    phase_angle = 2.0 * jnp.pi * frequency[:, None] * time_steps[None, :] / total_times
    edge_rows = (freq_index == 0) | (freq_index == half_count)
    cosine = jnp.where(edge_rows[:, None], jnp.cos(phase_angle) / math.sqrt(total_times), jnp.cos(phase_angle) * math.sqrt(2.0 / total_times))
    return jnp.where((freq_index > half_count)[:, None], jnp.sin(phase_angle) * math.sqrt(2.0 / total_times), cosine)

def shift_of(freq_index, total_times):
    half_count = total_times // 2
    frequency = jnp.where(freq_index <= half_count, freq_index, freq_index - half_count).astype(jnp.float32)
    return base_shift + time_coupling * (2.0 - 2.0 * jnp.cos(2.0 * jnp.pi * frequency / total_times))

def operate(field, north_values, south_values, time_shift, mass_c, north_coupling, south_coupling, east_coupling):
    east_values = jnp.roll(field, -1, -1)
    west_values = jnp.roll(field, 1, -1)
    west_coupling = jnp.roll(east_coupling, 1, -1)
    return (time_shift + mass_c) * field + north_coupling * (field - north_values) + south_coupling * (field - south_values) + east_coupling * (field - east_values) + west_coupling * (field - west_values)

def reference(states, mass_term, lat_coupling, lon_coupling):
    total_times = states.shape[1]
    transform = time_basis(total_times)
    spectral = jnp.einsum('kt,ftrl->fkrl', transform, states, precision=lax.Precision.HIGHEST)
    zero_row = jnp.zeros((1, lat_coupling.shape[1]), jnp.float32)
    south_coupling = jnp.concatenate([zero_row, lat_coupling[:-1]], 0)

    def solve_one(inputs):
        fields_block, freq_index = inputs
        time_shift = shift_of(freq_index, total_times)
        lower_bound = time_shift + mass_low
        upper_bound = time_shift + mass_high + 8.0 * coupling_high
        center_value = (upper_bound + lower_bound) / 2.0
        half_width = (upper_bound - lower_bound) / 2.0
        ratio_bound = center_value / half_width

        def sweep_once(sweep_index, loop_state):
            iterate, residual, direction, ratio_now = loop_state
            zero_rows = jnp.zeros_like(direction[:, :1])
            north_values = jnp.concatenate([direction[:, 1:], zero_rows], 1)
            south_values = jnp.concatenate([zero_rows, direction[:, :-1]], 1)
            image_field = operate(direction, north_values, south_values, time_shift, mass_term, lat_coupling, south_coupling, lon_coupling)
            iterate = iterate + direction
            residual = residual - image_field
            ratio_next = 1.0 / (2.0 * ratio_bound - ratio_now)
            direction = ratio_next * ratio_now * direction + 2.0 * ratio_next / half_width * residual
            return (iterate, residual, direction, ratio_next)
        start = (jnp.zeros_like(fields_block), fields_block, fields_block / center_value, 1.0 / ratio_bound)
        iterate, residual, direction, ratio_now = lax.fori_loop(0, SWEEPS, sweep_once, start)
        return iterate + direction
    solved = lax.map(solve_one, (jnp.moveaxis(spectral, 1, 0), jnp.arange(total_times, dtype=jnp.int32)))
    solved = jnp.moveaxis(solved, 0, 1)
    return jnp.einsum('kt,fkrl->ftrl', transform, solved, precision=lax.Precision.HIGHEST)
```

```python
import math

import jax
import jax.numpy as jnp
import numpy as np
from jax import lax
from jax.experimental import pallas as pl
from jax.experimental.pallas import tpu as pltpu
from jax.sharding import PartitionSpec as P

SWEEPS = 16
HALO = SWEEPS
LEVELS = 4
CHUNK = 37
PAD = 8
LANES = 128
SUB = 8

mass_low = 0.005
mass_high = 0.05
coupling_high = 2.0
base_shift = 0.002
time_coupling = 0.05
CENTER = (mass_low + mass_high + 8.0 * coupling_high) / 2.0
DELTA = (mass_high + 8.0 * coupling_high - mass_low) / 2.0


def frequencies(times):
    index = np.arange(times)
    return np.where(index <= times // 2, index, index - times // 2).astype(np.float64)


def time_basis(times):
    freq = frequencies(times)
    index = np.arange(times)
    angle = 2.0 * np.pi * freq[:, None] * np.arange(times)[None, :] / times
    edge = ((index == 0) | (index == times // 2))[:, None]
    cosine = np.cos(angle) * np.where(edge, math.sqrt(1.0 / times), math.sqrt(2.0 / times))
    sine = np.sin(angle) * math.sqrt(2.0 / times)
    return np.where((index > times // 2)[:, None], sine, cosine)


def weights(times):
    shift = base_shift + time_coupling * (2.0 - 2.0 * np.cos(2.0 * np.pi * frequencies(times) / times))
    sigma = (shift + CENTER) / DELTA
    second = [np.ones_like(sigma), 2.0 * sigma]
    first = [np.ones_like(sigma), sigma]
    for _ in range(SWEEPS):
        second.append(2.0 * sigma * second[-1] - second[-2])
        first.append(2.0 * sigma * first[-1] - first[-2])
    rows = [2.0 * second[SWEEPS - j] / (DELTA * first[SWEEPS + 1]) for j in range(SWEEPS + 1)]
    return 0.5 * np.stack(rows)


def padded_length(width):
    steps = -(-(width + LEVELS - 1) // CHUNK) * CHUNK
    return -(-(PAD + steps + 1) // SUB) * SUB


def run_sweeps(width, times, b_ref, p_ref, q_ref, e_ref, diag_ref, lon_ref, lat_ref, c_ref):
    lanes = b_ref.shape[1]
    trips = -(-(width + LEVELS - 1) // CHUNK)

    def rows(ref, j):
        return ref[pl.ds(pl.multiple_of(j * times, SUB), times), :]

    def wide(ref, j):
        return jnp.broadcast_to(ref[pl.ds(j, 1), :], (times, lanes))

    kept = [(l, -l - k) for l in range(LEVELS) for k in (1, 0)]
    kept += [(name, -k) for name in ("rhs", "diag", "lat") for k in range(1, LEVELS)]
    kept += [("lon", -k) for k in range(1, LEVELS + 1)]

    def one_pass(index, carry):
        c = [
            c_ref[pl.ds(pl.multiple_of((SWEEPS - 1 - LEVELS * index - l) * times, SUB), times), :]
            for l in range(LEVELS)
        ]

        def trip(number, held):
            start = PAD + number * CHUNK
            held = iter(held)
            u = [dict() for _ in range(LEVELS + 1)]
            rhs, diag, lat, lon = {}, {}, {}, {}
            for table, at in kept:
                (u[table] if isinstance(table, int) else dict(rhs=rhs, diag=diag, lat=lat, lon=lon)[table])[at] = next(held)
            for s in range(CHUNK):
                u[0][s + 1] = rows(p_ref, start + s + 1)
                rhs[s] = rows(b_ref, start + s)
                diag[s] = wide(diag_ref, start + s)
                lat[s] = wide(lat_ref, start + s)
                lon[s] = wide(lon_ref, start + s)
                for l in range(LEVELS):
                    i = s - l
                    v = u[l]
                    older = rows(q_ref, start + s) if l == 0 else u[l - 1][i]
                    near = v[i]
                    south = pltpu.roll(lat[i] * near, 1, 1)
                    north = lat[i] * pltpu.roll(near, lanes - 1, 1)
                    total = (c[l] * rhs[i] - older) + (diag[i] * near + lon[i - 1] * v[i - 1])
                    total = total + (north + south)
                    u[l + 1][i] = total + lon[i] * v[i + 1]
                q_ref[pl.ds(pl.multiple_of((start + s - LEVELS + 2) * times, SUB), times), :] = u[LEVELS - 1][
                    s - LEVELS + 2
                ]
                done = s - LEVELS + 1
                where = pl.ds(pl.multiple_of((start + done) * times, SUB), times)
                p_ref[where, :] = u[LEVELS][done]
                e_ref[where, :] = u[LEVELS][done] - u[LEVELS - 2][done]
            tables = dict(rhs=rhs, diag=diag, lat=lat, lon=lon)
            return tuple((u[table] if isinstance(table, int) else tables[table])[CHUNK + at] for table, at in kept)

        zero = jnp.zeros((times, lanes), jnp.float32)
        lax.fori_loop(0, trips, trip, tuple(rows(p_ref, PAD) if at == (0, 0) else zero for at in kept))
        return carry

    lax.fori_loop(0, SWEEPS // LEVELS, one_pass, 0)


R2 = math.sqrt(0.5)


def spread(x):
    e1, e2, e3 = x[1] + x[7], x[2] + x[6], x[3] + x[5]
    o1, o2, o3 = x[1] - x[7], x[2] - x[6], x[3] - x[5]
    a, b = x[0] + x[4], x[0] - x[4]
    p, m, q, n = e1 + e3, R2 * (e1 - e3), a + e2, R2 * (o1 + o3)
    return [q + p, b + m, a - e2, b - m, q - p, n + o2, o1 - o3, n - o2]


def gather_times(v):
    s, d = v[0] + v[4], v[0] - v[4]
    m, p, n = R2 * (v[1] - v[3]), v[1] + v[3], R2 * (v[5] + v[7])
    sv, g, h = s + v[2], s - v[2], v[5] - v[7]
    dp, dm, np_, nm = d + m, d - m, n + v[6], n - v[6]
    return [sv + p, dp + np_, g + h, dm + nm, sv - p, dm - nm, g - h, dp - np_]


def halo_group(pieces, width):
    lane = lax.broadcasted_iota(jnp.int32, (SUB, LANES), 1)
    groups = LANES // width
    out = []
    for q in range(groups):
        tile = None
        for g, piece in enumerate(pieces):
            moved = piece if g == q else pltpu.roll(piece, (width * (g - q)) % LANES, 1)
            tile = moved if tile is None else jnp.where(lane < width * g, tile, moved)
        out.append(tile)
    return out


def pack_kernel(width, band_ref, s_ref, m_ref, y_ref, x_ref, send_ref, coef_ref):
    bands = s_ref.shape[2] // width
    rl = s_ref.shape[1]
    lane = lax.broadcasted_iota(jnp.int32, (rl, LANES), 1)
    small = lax.broadcasted_iota(jnp.int32, (SUB, LANES), 1)
    group = 2 * HALO

    def pack(west, east):
        both = pltpu.roll(jnp.where(lane < LANES // 2, east, west), HALO, 1)
        tile = None
        for q in range(rl // SUB):
            piece = both[q * SUB : (q + 1) * SUB]
            moved = piece if q == 0 else pltpu.roll(piece, group * q, 1)
            tile = moved if tile is None else jnp.where(small < group * q, tile, moved)
        return tile

    tiles = width // LANES
    total = bands * width
    for f in range(s_ref.shape[0]):
        for i in range(bands):
            for h in range(tiles):
                lo = i * width + h * LANES
                send_ref[i, f, h * rl : (h + 1) * rl, :] = s_ref[f, :, lo : lo + LANES]
            lo_w = (i * width - LANES) % total
            lo_e = ((i + 1) * width) % total
            send_ref[i, f, tiles * rl :, :] = pack(s_ref[f, :, lo_w : lo_w + LANES], s_ref[f, :, lo_e : lo_e + LANES])
    band = band_ref[0]
    lo = pl.multiple_of(band * width, LANES)
    lo_w = pl.multiple_of(lax.rem(band * width + (total - LANES), total), LANES)
    lo_e = pl.multiple_of(lax.rem((band + 1) * width, total), LANES)
    for n, ref in enumerate((m_ref, y_ref, x_ref)):
        for h in range(tiles):
            coef_ref[n, h * rl : (h + 1) * rl, :] = ref[:, pl.ds(lo + h * LANES, LANES)]
        coef_ref[n, tiles * rl :, :] = pack(ref[:, pl.ds(lo_w, LANES)], ref[:, pl.ds(lo_e, LANES)])


def finish_coefficients(m, y, x):
    scale = 2.0 / DELTA
    lane = lax.broadcasted_iota(jnp.int32, m.shape, 1)
    south = jnp.where(lane == 0, 0.0, pltpu.roll(y, 1, 1))
    west = pltpu.roll(x, 1, 0)
    diag = scale * (CENTER - m - (y + south) - (x + west))
    return diag, scale * x, jnp.where(lane == m.shape[1] - 1, 0.0, scale * y)


def coef_kernel(width, g_ref, diag_ref, lon_ref, lat_ref, t_ref, tile_ref):
    lats, count, _, _ = g_ref.shape
    tiles = width // LANES
    rl = (g_ref.shape[2] * LANES - 0) // (width + 2 * HALO)
    for n in range(count):
        for h in range(tiles):
            for l in range(lats):
                tile_ref[l * rl : (l + 1) * rl, :] = g_ref[l, n, h * rl : (h + 1) * rl, :]
            t_ref[n, HALO + h * LANES : HALO + (h + 1) * LANES, :] = tile_ref[...].T
    for l in range(lats):
        got = halo_group([g_ref[l, n, tiles * rl :, :] for n in range(count)], 2 * HALO)
        for q, piece in enumerate(got):
            tile_ref[l * rl + q * SUB : l * rl + (q + 1) * SUB, :] = piece
    turned = tile_ref[...].T
    for n in range(count):
        t_ref[n, :HALO, :] = turned[n * 2 * HALO : n * 2 * HALO + HALO]
        t_ref[n, HALO + width :, :] = turned[n * 2 * HALO + HALO : (n + 1) * 2 * HALO]
    out = finish_coefficients(t_ref[0], t_ref[1], t_ref[2])
    full = width + 2 * HALO
    for ref, value in zip((diag_ref, lon_ref, lat_ref), out):
        ref[:PAD, :] = jnp.zeros((PAD, ref.shape[1]), jnp.float32)
        ref[PAD : PAD + full, :] = value
        ref[PAD + full :, :] = jnp.zeros((ref.shape[0] - PAD - full, ref.shape[1]), jnp.float32)


def solve_kernel(width, first, g_ref, diag_ref, lon_ref, lat_ref, c_ref, out_ref, b_ref, p_ref, q_ref, e_ref, t_ref, tile_ref):
    full = width + 2 * HALO
    times = t_ref.shape[0]
    lats = g_ref.shape[0] // times
    tiles = width // LANES
    rl = t_ref.shape[2] // lats
    for t in range(times):
        for h in range(tiles):
            turned = jnp.concatenate([g_ref[t * lats + l, h * rl : (h + 1) * rl, :] for l in range(lats)], 0).T
            t_ref[t, HALO + h * LANES : HALO + (h + 1) * LANES, :] = turned
    per = LANES // (2 * HALO)
    for g in range(times // per):
        for l in range(lats):
            got = halo_group([g_ref[(g * per + n) * lats + l, tiles * rl :, :] for n in range(per)], 2 * HALO)
            for q, piece in enumerate(got):
                tile_ref[l * rl + q * SUB : l * rl + (q + 1) * SUB, :] = piece
        turned = tile_ref[...].T
        for n in range(per):
            t_ref[g * per + n, :HALO, :] = turned[n * 2 * HALO : n * 2 * HALO + HALO]
            t_ref[g * per + n, HALO + width :, :] = turned[n * 2 * HALO + HALO : (n + 1) * 2 * HALO]

    lanes = b_ref.shape[1]
    head = PAD * times
    tail = (PAD + full) * times
    for ref in (b_ref, p_ref):
        ref[:head, :] = jnp.zeros((head, lanes), jnp.float32)
        ref[tail:, :] = jnp.zeros((ref.shape[0] - tail, lanes), jnp.float32)
    q_ref[...] = jnp.zeros(q_ref.shape, jnp.float32)

    def to_frequencies(block, carry):
        lo = pl.multiple_of(block * SUB, SUB)
        v = spread([t_ref[t, pl.ds(lo, SUB), :] for t in range(times)])
        for k in range(times):
            where = pl.ds((PAD + lo) * times + k, SUB, stride=times)
            b_ref[where, :] = v[k]
            p_ref[where, :] = v[k] * float(first[k])
        return carry

    lax.fori_loop(0, full // SUB, to_frequencies, 0)
    run_sweeps(full, times, b_ref, p_ref, q_ref, e_ref, diag_ref, lon_ref, lat_ref, c_ref)

    def to_times(block, carry):
        lo = pl.multiple_of(block * SUB, SUB)
        base = (PAD + HALO + lo) * times
        v = gather_times([e_ref[pl.ds(base + k, SUB, stride=times), :] for k in range(times)])
        for t in range(times):
            t_ref[t, pl.ds(lo, SUB), :] = v[t]
        return carry

    lax.fori_loop(0, width // SUB, to_times, 0)
    for t in range(times):
        for h in range(tiles):
            turned = t_ref[t, h * LANES : (h + 1) * LANES, :].T
            for l in range(lats):
                out_ref[t * lats + l, h * rl : (h + 1) * rl, :] = turned[l * rl : (l + 1) * rl]


def sweep_kernel(width, b_in, diag_ref, lon_ref, lat_ref, c_ref, e_ref, p_ref, q_ref):
    times = c_ref.shape[0] // (SWEEPS + 1)
    top = c_ref[SWEEPS * times :, :]

    def begin(j, carry):
        where = pl.ds(pl.multiple_of(j * times, SUB), times)
        p_ref[where, :] = top * b_in[where, :]
        return carry

    lax.fori_loop(0, b_in.shape[0] // times, begin, 0)
    q_ref[...] = jnp.zeros(q_ref.shape, jnp.float32)
    run_sweeps(width, times, b_in, p_ref, q_ref, e_ref, diag_ref, lon_ref, lat_ref, c_ref)


VMEM = pl.BlockSpec(memory_space=pltpu.VMEM)
SMEM = pl.BlockSpec(memory_space=pltpu.SMEM)


def params(limit=None):
    return pltpu.CompilerParams(vmem_limit_bytes=limit)


def gather_rows(block, axis):
    count = lax.axis_size(axis)
    me = lax.axis_index(axis)
    got = block[None]
    step = 1
    while step < count:
        other = lax.ppermute(got, axis, [(i, i ^ step) for i in range(count)])
        low = (me & step) == 0
        got = jnp.concatenate([jnp.where(low, got, other), jnp.where(low, other, got)], 0)
        step *= 2
    return got


def solve_packed(states, mass_term, lat_coupling, lon_coupling):
    fields, _, rl, nlon = states.shape
    times, lats = lax.axis_size("tm"), lax.axis_size("lat")
    width = nlon // times
    rows = rl * lats
    full = width + 2 * HALO
    height = full * rl // LANES
    length = padded_length(full)
    f32 = jnp.float32
    band = lax.axis_index("tm").astype(jnp.int32).reshape(1)
    send, coef = pl.pallas_call(
        lambda *refs: pack_kernel(width, *refs),
        out_shape=(
            jax.ShapeDtypeStruct((times, lats, height, LANES), f32),
            jax.ShapeDtypeStruct((3, height, LANES), f32),
        ),
        in_specs=[SMEM] + [VMEM] * 4,
        out_specs=(VMEM, VMEM),
        cost_estimate=pl.CostEstimate(flops=0, transcendentals=0, bytes_accessed=8 * states.size),
        name="pack",
    )(band, states.reshape(fields, rl, nlon), mass_term, lat_coupling, lon_coupling)
    coefs = gather_rows(coef, "lat")
    got = lax.all_to_all(send.reshape(times * lats, height, LANES), ("tm", "lat"), 0, 0, tiled=True)
    line = jax.ShapeDtypeStruct((length, rows), f32)
    diag, lon, lat = pl.pallas_call(
        lambda *refs: coef_kernel(width, *refs),
        out_shape=(line,) * 3,
        in_specs=[VMEM],
        out_specs=(VMEM,) * 3,
        scratch_shapes=[pltpu.VMEM((3, full, rows), f32), pltpu.VMEM((rows, LANES), f32)],
        cost_estimate=pl.CostEstimate(flops=30 * full * rows, transcendentals=0, bytes_accessed=24 * full * rows),
        name="coefficients",
    )(coefs)
    basis = time_basis(times)
    scale = np.max(np.abs(basis), 1) ** 2
    scale = np.where(scale > 1.5 / times, 2.0 / times, 1.0 / times)
    c = weights(times) * scale[None, :]
    c_rows = jnp.broadcast_to(jnp.asarray(c.reshape(-1, 1), f32), ((SWEEPS + 1) * times, rows))
    slab = pltpu.VMEM((length * times, rows), f32)
    out = pl.pallas_call(
        lambda *refs: solve_kernel(width, c[SWEEPS], *refs),
        out_shape=jax.ShapeDtypeStruct((times * lats, width * rl // LANES, LANES), f32),
        in_specs=[VMEM] * 5,
        out_specs=VMEM,
        scratch_shapes=[slab] * 4 + [pltpu.VMEM((times, full, rows), f32), pltpu.VMEM((rows, LANES), f32)],
        cost_estimate=pl.CostEstimate(
            flops=12 * SWEEPS * full * times * rows, transcendentals=0, bytes_accessed=8 * full * times * rows
        ),
        name="solve",
    )(got, diag, lon, lat, c_rows)
    back = lax.all_to_all(out, ("tm", "lat"), 0, 0, tiled=True)
    back = back.reshape(times, lats, width // LANES, rl, LANES)
    return back.transpose(1, 3, 0, 2, 4).reshape(fields, 1, rl, nlon)


def solve_general(states, mass_term, lat_coupling, lon_coupling):
    fields, tl, rl, nlon = states.shape
    tm, lats = lax.axis_size("tm"), lax.axis_size("lat")
    times, rows, parts = tl * tm, rl * lats, lats // fields
    width = nlon // (tm * parts)
    full = width + 2 * HALO
    length = padded_length(full)
    f32 = jnp.float32

    def wrapped(a):
        return jnp.concatenate([a[..., nlon - HALO :], a, a[..., :HALO]], -1)

    wide = wrapped(states)
    bands = jnp.stack([wide[..., n * width : n * width + full] for n in range(tm * parts)])
    bands = bands.reshape(tm, parts, fields, tl, rl, full).transpose(0, 2, 1, 3, 4, 5)
    got = lax.all_to_all(bands.reshape(tm * lats, tl, rl, full), ("tm", "lat"), 0, 0, tiled=True)
    field = got.reshape(tm, lats, tl, rl, full).transpose(4, 0, 2, 1, 3).reshape(full, times, rows)
    basis = jnp.asarray(time_basis(times), f32)
    b = jnp.einsum("kt,jtr->jkr", basis, field, precision=lax.Precision.HIGHEST)
    coef = wrapped(jnp.stack([mass_term, lat_coupling, lon_coupling]))
    first = lax.axis_index("tm") * parts
    mine = jnp.stack([lax.dynamic_slice_in_dim(coef, (first + n) * width, full, 2) for n in range(parts)])
    mine = jnp.broadcast_to(mine[None], (fields,) + mine.shape).reshape(lats, 3, rl, full)
    all_rows = lax.all_to_all(mine, "lat", 0, 0, tiled=True)
    m, y, x = all_rows.transpose(1, 3, 0, 2).reshape(3, full, rows)
    scale = 2.0 / DELTA
    south = jnp.concatenate([jnp.zeros((full, 1), f32), y[:, :-1]], 1)
    diag = scale * (CENTER - m - (y + south) - (x + jnp.roll(x, 1, 0)))
    lat = scale * jnp.concatenate([y[:, :-1], jnp.zeros((full, 1), f32)], 1)
    ends = ((PAD, length - PAD - full), (0, 0))
    diag, lon, lat = (jnp.pad(a, ends) for a in (diag, scale * x, lat))
    b = jnp.pad(b, (ends[0], (0, 0), (0, 0))).reshape(length * times, rows)
    c = weights(times)
    c_rows = jnp.broadcast_to(jnp.asarray(c.reshape(-1, 1), f32), ((SWEEPS + 1) * times, rows))
    slab = pltpu.VMEM((length * times, rows), f32)
    solved = pl.pallas_call(
        lambda *refs: sweep_kernel(full, *refs),
        out_shape=jax.ShapeDtypeStruct((length * times, rows), f32),
        in_specs=[VMEM] * 5,
        out_specs=VMEM,
        scratch_shapes=[slab] * 2,
        name="sweeps",
    )(b, diag, lon, lat, c_rows)
    solved = solved.reshape(length, times, rows)[PAD + HALO : PAD + HALO + width]
    field = jnp.einsum("kt,jkr->jtr", basis, solved, precision=lax.Precision.HIGHEST)
    field = field.reshape(width, tm, tl, lats, rl).transpose(1, 3, 2, 4, 0).reshape(tm * lats, tl, rl, width)
    back = lax.all_to_all(field, ("tm", "lat"), 0, 0, tiled=True)
    back = back.reshape(tm, fields, parts, tl, rl, width).transpose(1, 3, 4, 0, 2, 5)
    return back.reshape(fields, tl, rl, nlon)


def per_device(states, mass_term, lat_coupling, lon_coupling):
    fields, tl, rl, nlon = states.shape
    tm, lats = lax.axis_size("tm"), lax.axis_size("lat")
    packed = tl == 1 and tm == SUB and lats == fields and rl * lats == LANES
    packed = packed and nlon % (tm * LANES) == 0 and 2 * HALO * rl == SUB * LANES
    plan = solve_packed if packed else solve_general
    return plan(states, mass_term, lat_coupling, lon_coupling)


def solution(mesh):
    placed = (P(None, "tm", "lat", None), P("lat", None), P("lat", None), P("lat", None))
    return jax.shard_map(
        per_device,
        mesh=mesh,
        in_specs=placed,
        out_specs=P(None, "tm", "lat", None),
        check_vma=False,
    )
```

```python
import math

import jax
import jax.numpy as jnp
import numpy as np
from jax import lax
from jax.experimental import pallas as pl
from jax.experimental.pallas import tpu as pltpu
from jax.sharding import PartitionSpec as P

SWEEPS = 16
HALO = SWEEPS
PACK_BANDS = 2
PAD = 8
LANES = 128
SUB = 8

mass_low = 0.005
mass_high = 0.05
coupling_high = 2.0
base_shift = 0.002
time_coupling = 0.05
CENTER = (mass_low + mass_high + 8.0 * coupling_high) / 2.0
DELTA = (mass_high + 8.0 * coupling_high - mass_low) / 2.0


def frequencies(times):
    index = np.arange(times)
    return np.where(index <= times // 2, index, index - times // 2).astype(np.float64)


def time_basis(times):
    freq = frequencies(times)
    index = np.arange(times)
    angle = 2.0 * np.pi * freq[:, None] * np.arange(times)[None, :] / times
    edge = ((index == 0) | (index == times // 2))[:, None]
    cosine = np.cos(angle) * np.where(edge, math.sqrt(1.0 / times), math.sqrt(2.0 / times))
    sine = np.sin(angle) * math.sqrt(2.0 / times)
    return np.where((index > times // 2)[:, None], sine, cosine)


def weights(times):
    shift = base_shift + time_coupling * (2.0 - 2.0 * np.cos(2.0 * np.pi * frequencies(times) / times))
    sigma = (shift + CENTER) / DELTA
    second = [np.ones_like(sigma), 2.0 * sigma]
    first = [np.ones_like(sigma), sigma]
    for _ in range(SWEEPS):
        second.append(2.0 * sigma * second[-1] - second[-2])
        first.append(2.0 * sigma * first[-1] - first[-2])
    rows = [2.0 * second[SWEEPS - j] / (DELTA * first[SWEEPS + 1]) for j in range(SWEEPS + 1)]
    return 0.5 * np.stack(rows)


def padded_length(width):
    return -(-(PAD + width + 1) // SUB) * SUB


def run_sweeps(columns, rows, b_ref, p_ref, q_ref, diag_ref, lon_ref, lat_ref, c_ref):
    stride = rows + PAD
    turn = SUB

    def sweep(c, new_ref, old_ref, place_ref, last=False, gain=None):
        for block in range(rows // SUB):

            def at(ref, column, shift=0):
                lo = column * stride + PAD + block * SUB + shift
                return ref[lo : lo + SUB, :]

            def coef(ref, column):
                lo = column * rows + block * SUB
                return ref[lo : lo + SUB, :]

            final = columns - 1
            for n in range(columns):
                near = at(new_ref, n)
                east = at(new_ref, n + 1) if n < final else pltpu.roll(at(new_ref, 0), LANES - turn, 1)
                west = at(new_ref, n - 1) if n > 0 else pltpu.roll(at(new_ref, final), turn, 1)
                lon_west = coef(lon_ref, n - 1) if n > 0 else pltpu.roll(coef(lon_ref, final), turn, 1)
                image = (coef(diag_ref, n) * near + coef(lon_ref, n) * east) + lon_west * west
                image = image + at(lat_ref, n) * at(new_ref, n, 1) + at(lat_ref, n, -1) * at(new_ref, n, -1)
                if gain is not None:
                    image = gain * image
                total = c * at(b_ref, n) + image
                if old_ref is not None:
                    total = total - at(old_ref, n)
                if last:
                    total = total - at(old_ref, n)
                lo = n * stride + PAD + block * SUB
                place_ref[lo : lo + SUB, :] = total

    def wide(degree):
        return jnp.broadcast_to(c_ref[pl.ds(degree, 1), :], (SUB, LANES))

    top = wide(SWEEPS)
    sweep(wide(SWEEPS - 1), b_ref, None, q_ref, gain=top)
    sweep(wide(SWEEPS - 2) - top, q_ref, None, p_ref)

    def pair(index, carry):
        sweep(wide(SWEEPS - 3 - 2 * index), p_ref, q_ref, q_ref)
        sweep(wide(SWEEPS - 4 - 2 * index), q_ref, p_ref, p_ref)
        return carry

    lax.fori_loop(0, SWEEPS // 2 - 2, pair, 0)
    sweep(wide(1), p_ref, q_ref, q_ref)
    sweep(wide(0), q_ref, p_ref, p_ref, last=True)


R2 = math.sqrt(0.5)


def spread(x):
    e1, e2, e3 = x[1] + x[7], x[2] + x[6], x[3] + x[5]
    o1, o2, o3 = x[1] - x[7], x[2] - x[6], x[3] - x[5]
    a, b = x[0] + x[4], x[0] - x[4]
    p, m, q, n = e1 + e3, R2 * (e1 - e3), a + e2, R2 * (o1 + o3)
    return [q + p, b + m, a - e2, b - m, q - p, n + o2, o1 - o3, n - o2]


def gather_times(v):
    s, d = v[0] + v[4], v[0] - v[4]
    m, p, n = R2 * (v[1] - v[3]), v[1] + v[3], R2 * (v[5] + v[7])
    sv, g, h = s + v[2], s - v[2], v[5] - v[7]
    dp, dm, np_, nm = d + m, d - m, n + v[6], n - v[6]
    return [sv + p, dp + np_, g + h, dm + nm, sv - p, dm - nm, g - h, dp - np_]


def halo_group(pieces, width):
    lane = lax.broadcasted_iota(jnp.int32, (SUB, LANES), 1)
    groups = LANES // width
    out = []
    for q in range(groups):
        tile = None
        for g, piece in enumerate(pieces):
            moved = piece if g == q else pltpu.roll(piece, (width * (g - q)) % LANES, 1)
            tile = moved if tile is None else jnp.where(lane < width * g, tile, moved)
        out.append(tile)
    return out


def pack_halo(west, east):
    rl = west.shape[0]
    lane = lax.broadcasted_iota(jnp.int32, (rl, LANES), 1)
    small = lax.broadcasted_iota(jnp.int32, (SUB, LANES), 1)
    both = pltpu.roll(jnp.where(lane < LANES // 2, east, west), HALO, 1)
    tile = None
    for q in range(rl // SUB):
        piece = both[q * SUB : (q + 1) * SUB]
        moved = piece if q == 0 else pltpu.roll(piece, 2 * HALO * q, 1)
        tile = moved if tile is None else jnp.where(small < 2 * HALO * q, tile, moved)
    return tile


def pack_kernel(width, s_ref, west_ref, east_ref, send_ref):
    fields, rl, total = s_ref.shape
    tiles = width // LANES
    bands = total // width
    for f in range(fields):
        for i in range(bands):
            lo = i * width
            for h in range(tiles):
                send_ref[i, f, h * rl : (h + 1) * rl, :] = s_ref[f, :, lo + h * LANES : lo + (h + 1) * LANES]
            west = west_ref[f] if i == 0 else s_ref[f, :, lo - LANES : lo]
            east = east_ref[f] if i == bands - 1 else s_ref[f, :, lo + width : lo + width + LANES]
            send_ref[i, f, tiles * rl :, :] = pack_halo(west, east)


def pack_coef_kernel(width, band_ref, m_ref, y_ref, x_ref, coef_ref):
    rl, total = m_ref.shape
    tiles = width // LANES
    band = band_ref[0]
    lo = pl.multiple_of(band * width, LANES)
    lo_w = pl.multiple_of(lax.rem(band * width + (total - LANES), total), LANES)
    lo_e = pl.multiple_of(lax.rem((band + 1) * width, total), LANES)
    for n, ref in enumerate((m_ref, y_ref, x_ref)):
        for h in range(tiles):
            coef_ref[n, h * rl : (h + 1) * rl, :] = ref[:, pl.ds(lo + h * LANES, LANES)]
        coef_ref[n, tiles * rl :, :] = pack_halo(ref[:, pl.ds(lo_w, LANES)], ref[:, pl.ds(lo_e, LANES)])


def unpack_kernel(width, g_ref, out_ref):
    fields, rl, total = out_ref.shape
    for i in range(total // width):
        for f in range(fields):
            for h in range(width // LANES):
                lo = i * width + h * LANES
                out_ref[f, :, lo : lo + LANES] = g_ref[i * fields + f, h * rl : (h + 1) * rl, :]


def finish_coefficients(m, y, x):
    scale = 2.0 / DELTA
    lane = lax.broadcasted_iota(jnp.int32, m.shape, 1)
    south = jnp.where(lane == 0, 0.0, pltpu.roll(y, 1, 1))
    west = pltpu.roll(x, 1, 0)
    diag = scale * (CENTER - m - (y + south) - (x + west))
    return diag, scale * x, scale * y


def coef_kernel(width, times, g_ref, diag_ref, lon_ref, lat_ref, t_ref, tile_ref):
    lats, count, _, _ = g_ref.shape
    tiles = width // LANES
    rl = g_ref.shape[2] * LANES // (width + 2 * HALO)
    for n in range(count):
        for h in range(tiles):
            for l in range(lats):
                tile_ref[l * rl : (l + 1) * rl, :] = g_ref[l, n, h * rl : (h + 1) * rl, :]
            t_ref[n, HALO + h * LANES : HALO + (h + 1) * LANES, :] = tile_ref[...].T
    for l in range(lats):
        got = halo_group([g_ref[l, n, tiles * rl :, :] for n in range(count)], 2 * HALO)
        for q, piece in enumerate(got):
            tile_ref[l * rl + q * SUB : l * rl + (q + 1) * SUB, :] = piece
    turned = tile_ref[...].T
    for n in range(count):
        t_ref[n, :HALO, :] = turned[n * 2 * HALO : n * 2 * HALO + HALO]
        t_ref[n, HALO + width :, :] = turned[n * 2 * HALO + HALO : (n + 1) * 2 * HALO]
    for n, value in enumerate(finish_coefficients(t_ref[0], t_ref[1], t_ref[2])):
        t_ref[n] = value
    rows = t_ref.shape[2]
    groups = LANES // times
    columns = (width + 2 * HALO) // groups
    stride = rows + PAD
    zero = jnp.zeros((PAD, LANES), jnp.float32)
    for c in range(columns):
        for n, ref in enumerate((diag_ref, lon_ref, lat_ref)):
            picked = [t_ref[n, g * columns + c : g * columns + c + 1, :] for g in range(groups)]
            turned = jnp.concatenate([jnp.broadcast_to(row, (times, rows)) for row in picked], 0).T
            if n == 2:
                ref[c * stride : c * stride + PAD, :] = zero
                ref[c * stride + PAD : (c + 1) * stride, :] = turned
            else:
                ref[c * rows : (c + 1) * rows, :] = turned
    lat_ref[columns * stride :, :] = zero


def solve_kernel(width, g_ref, diag_ref, lon_ref, lat_ref, c_ref, out_ref, b_ref, p_ref, q_ref, line_ref, t_ref, tile_ref):
    full = width + 2 * HALO
    times, _, rows = t_ref.shape
    lats = g_ref.shape[0] // times
    tiles = width // LANES
    rl = rows // lats
    groups = LANES // times
    columns = full // groups
    stride = rows + PAD
    for t in range(times):
        for h in range(tiles):
            turned = jnp.concatenate([g_ref[t * lats + l, h * rl : (h + 1) * rl, :] for l in range(lats)], 0).T
            t_ref[t, HALO + h * LANES : HALO + (h + 1) * LANES, :] = turned
    per = LANES // (2 * HALO)
    for g in range(times // per):
        for l in range(lats):
            got = halo_group([g_ref[(g * per + n) * lats + l, tiles * rl :, :] for n in range(per)], 2 * HALO)
            for q, piece in enumerate(got):
                tile_ref[l * rl + q * SUB : l * rl + (q + 1) * SUB, :] = piece
        turned = tile_ref[...].T
        for n in range(per):
            t_ref[g * per + n, :HALO, :] = turned[n * 2 * HALO : n * 2 * HALO + HALO]
            t_ref[g * per + n, HALO + width :, :] = turned[n * 2 * HALO + HALO : (n + 1) * 2 * HALO]

    zero = jnp.zeros((PAD, LANES), jnp.float32)
    for ref in (b_ref, p_ref, q_ref):
        for c in range(columns + 1):
            ref[c * stride : c * stride + PAD, :] = zero

    def to_frequencies(block, carry):
        lo = pl.multiple_of(block * SUB, SUB)
        v = spread([t_ref[t, pl.ds(lo, SUB), :] for t in range(times)])
        for k in range(times):
            line_ref[pl.ds(lo * times + k, SUB, stride=times), :] = v[k]
        return carry

    lax.fori_loop(0, full // SUB, to_frequencies, 0)

    def place(group, column):
        lo = (group * columns + column) * times
        return slice(lo, lo + times)

    for c in range(columns):
        turned = jnp.concatenate([line_ref[place(g, c), :] for g in range(groups)], 0).T
        b_ref[c * stride + PAD : (c + 1) * stride, :] = turned
    run_sweeps(columns, rows, b_ref, p_ref, q_ref, diag_ref, lon_ref, lat_ref, c_ref)
    for c in range(columns):
        turned = p_ref[c * stride + PAD : (c + 1) * stride, :].T
        for g in range(groups):
            line_ref[place(g, c), :] = turned[g * times : (g + 1) * times]

    def to_times(block, carry):
        lo = pl.multiple_of(block * SUB, SUB)
        base = (HALO + lo) * times
        v = gather_times([line_ref[pl.ds(base + k, SUB, stride=times), :] for k in range(times)])
        for t in range(times):
            t_ref[t, pl.ds(lo, SUB), :] = v[t]
        return carry

    lax.fori_loop(0, width // SUB, to_times, 0)
    for t in range(times):
        for h in range(tiles):
            turned = t_ref[t, h * LANES : (h + 1) * LANES, :].T
            for l in range(lats):
                out_ref[t * lats + l, h * rl : (h + 1) * rl, :] = turned[l * rl : (l + 1) * rl]


def sweep_kernel(width, b_ref, diag_ref, lon_ref, lat_ref, c_ref, p_ref, q_ref):
    times = c_ref.shape[0] // (SWEEPS + 1)
    lanes = b_ref.shape[1]

    def rows(j):
        return pl.ds(pl.multiple_of(j * times, SUB), times)

    def wide(ref, j):
        return jnp.broadcast_to(ref[pl.ds(j, 1), :], (times, lanes))

    def begin(j, carry):
        p_ref[rows(j), :] = c_ref[SWEEPS * times :, :] * b_ref[rows(j), :]
        q_ref[rows(j), :] = jnp.zeros((times, lanes), jnp.float32)
        return carry

    lax.fori_loop(0, b_ref.shape[0] // times, begin, 0)

    def sweep(degree, new_ref, old_ref, last=False):
        def step(j, carry):
            j = j + PAD
            near = new_ref[rows(j), :]
            image = wide(diag_ref, j) * near + wide(lon_ref, j) * new_ref[rows(j + 1), :]
            image = image + wide(lon_ref, j - 1) * new_ref[rows(j - 1), :]
            lat = wide(lat_ref, j)
            image = image + lat * pltpu.roll(near, lanes - 1, 1) + pltpu.roll(lat * near, 1, 1)
            older = old_ref[rows(j), :]
            total = c_ref[rows(degree), :] * b_ref[rows(j), :] + image - older
            old_ref[rows(j), :] = total - older if last else total
            return carry

        lax.fori_loop(0, width, step, 0)

    def pair(index, carry):
        sweep(SWEEPS - 1 - 2 * index, p_ref, q_ref)
        sweep(SWEEPS - 2 - 2 * index, q_ref, p_ref)
        return carry

    lax.fori_loop(0, SWEEPS // 2 - 1, pair, 0)
    sweep(1, p_ref, q_ref)
    sweep(0, q_ref, p_ref, True)


VMEM = pl.BlockSpec(memory_space=pltpu.VMEM)
SMEM = pl.BlockSpec(memory_space=pltpu.SMEM)


def params(limit=None):
    return pltpu.CompilerParams(vmem_limit_bytes=limit)


def gather_rows(block, axis):
    count = lax.axis_size(axis)
    me = lax.axis_index(axis)
    got = block[None]
    step = 1
    while step < count:
        other = lax.ppermute(got, axis, [(i, i ^ step) for i in range(count)])
        low = (me & step) == 0
        got = jnp.concatenate([jnp.where(low, got, other), jnp.where(low, other, got)], 0)
        step *= 2
    return got


def solve_packed(states, mass_term, lat_coupling, lon_coupling):
    fields, _, rl, nlon = states.shape
    times, lats = lax.axis_size("tm"), lax.axis_size("lat")
    width = nlon // times
    rows = rl * lats
    full = width + 2 * HALO
    height = full * rl // LANES
    f32 = jnp.float32
    step = PACK_BANDS * width
    tiles = nlon // LANES
    send = pl.pallas_call(
        lambda *refs: pack_kernel(width, *refs),
        grid=(times // PACK_BANDS,),
        out_shape=jax.ShapeDtypeStruct((times, lats, height, LANES), f32),
        in_specs=[
            pl.BlockSpec((fields, rl, step), lambda i: (0, 0, i)),
            pl.BlockSpec((fields, rl, LANES), lambda i: (0, 0, (i * (step // LANES) + tiles - 1) % tiles)),
            pl.BlockSpec((fields, rl, LANES), lambda i: (0, 0, ((i + 1) * (step // LANES)) % tiles)),
        ],
        out_specs=pl.BlockSpec((PACK_BANDS, lats, height, LANES), lambda i: (i, 0, 0, 0)),
        cost_estimate=pl.CostEstimate(flops=0, transcendentals=0, bytes_accessed=8 * states.size),
        compiler_params=params(16 << 20),
        name="pack",
    )(*[states.reshape(fields, rl, nlon)] * 3)
    band = lax.axis_index("tm").astype(jnp.int32).reshape(1)
    coef = pl.pallas_call(
        lambda *refs: pack_coef_kernel(width, *refs),
        out_shape=jax.ShapeDtypeStruct((3, height, LANES), f32),
        in_specs=[SMEM] + [VMEM] * 3,
        out_specs=VMEM,
        cost_estimate=pl.CostEstimate(flops=0, transcendentals=0, bytes_accessed=16 * mass_term.size),
        compiler_params=params(16 << 20),
        name="pack_coefficients",
    )(band, mass_term, lat_coupling, lon_coupling)
    coefs = gather_rows(coef, "lat")
    got = lax.all_to_all(send.reshape(times * lats, height, LANES), ("tm", "lat"), 0, 0, tiled=True)
    groups = LANES // times
    columns = full // groups
    slab = ((rows + PAD) * columns + PAD, LANES)
    flat = (rows * columns, LANES)
    diag, lon, lat = pl.pallas_call(
        lambda *refs: coef_kernel(width, times, *refs),
        out_shape=(jax.ShapeDtypeStruct(flat, f32),) * 2 + (jax.ShapeDtypeStruct(slab, f32),),
        in_specs=[VMEM],
        out_specs=(VMEM,) * 3,
        scratch_shapes=[pltpu.VMEM((3, full, rows), f32), pltpu.VMEM((rows, LANES), f32)],
        cost_estimate=pl.CostEstimate(flops=30 * full * rows, transcendentals=0, bytes_accessed=128 * full * rows),
        compiler_params=params(16 << 20),
        name="coefficients",
    )(coefs)
    basis = time_basis(times)
    scale = np.max(np.abs(basis), 1) ** 2
    scale = np.where(scale > 1.5 / times, 2.0 / times, 1.0 / times)
    c_rows = jnp.asarray(np.tile(weights(times) * scale[None, :], (1, groups)), f32)
    out = pl.pallas_call(
        lambda *refs: solve_kernel(width, *refs),
        out_shape=jax.ShapeDtypeStruct((times * lats, width * rl // LANES, LANES), f32),
        in_specs=[VMEM] * 5,
        out_specs=VMEM,
        scratch_shapes=[pltpu.VMEM(slab, f32)] * 3
        + [pltpu.VMEM((full * times, rows), f32), pltpu.VMEM((times, full, rows), f32), pltpu.VMEM((rows, LANES), f32)],
        cost_estimate=pl.CostEstimate(
            flops=12 * SWEEPS * full * times * rows, transcendentals=0, bytes_accessed=8 * full * times * rows
        ),
        compiler_params=params(24 << 20),
        name="solve",
    )(got, diag, lon, lat, c_rows)
    back = lax.all_to_all(out, ("tm", "lat"), 0, 0, tiled=True)
    result = pl.pallas_call(
        lambda *refs: unpack_kernel(width, *refs),
        out_shape=jax.ShapeDtypeStruct((fields, rl, nlon), f32),
        in_specs=[VMEM],
        out_specs=VMEM,
        cost_estimate=pl.CostEstimate(flops=0, transcendentals=0, bytes_accessed=8 * states.size),
        compiler_params=params(16 << 20),
        name="unpack",
    )(back)
    return result.reshape(states.shape)


def solve_general(states, mass_term, lat_coupling, lon_coupling):
    fields, tl, rl, nlon = states.shape
    tm, lats = lax.axis_size("tm"), lax.axis_size("lat")
    times, rows, parts = tl * tm, rl * lats, lats // fields
    width = nlon // (tm * parts)
    full = width + 2 * HALO
    length = padded_length(full)
    f32 = jnp.float32

    def wrapped(a):
        return jnp.concatenate([a[..., nlon - HALO :], a, a[..., :HALO]], -1)

    wide = wrapped(states)
    bands = jnp.stack([wide[..., n * width : n * width + full] for n in range(tm * parts)])
    bands = bands.reshape(tm, parts, fields, tl, rl, full).transpose(0, 2, 1, 3, 4, 5)
    got = lax.all_to_all(bands.reshape(tm * lats, tl, rl, full), ("tm", "lat"), 0, 0, tiled=True)
    field = got.reshape(tm, lats, tl, rl, full).transpose(4, 0, 2, 1, 3).reshape(full, times, rows)
    basis = jnp.asarray(time_basis(times), f32)
    b = jnp.einsum("kt,jtr->jkr", basis, field, precision=lax.Precision.HIGHEST)
    coef = wrapped(jnp.stack([mass_term, lat_coupling, lon_coupling]))
    first = lax.axis_index("tm") * parts
    mine = jnp.stack([lax.dynamic_slice_in_dim(coef, (first + n) * width, full, 2) for n in range(parts)])
    mine = jnp.broadcast_to(mine[None], (fields,) + mine.shape).reshape(lats, 3, rl, full)
    all_rows = lax.all_to_all(mine, "lat", 0, 0, tiled=True)
    m, y, x = all_rows.transpose(1, 3, 0, 2).reshape(3, full, rows)
    scale = 2.0 / DELTA
    south = jnp.concatenate([jnp.zeros((full, 1), f32), y[:, :-1]], 1)
    diag = scale * (CENTER - m - (y + south) - (x + jnp.roll(x, 1, 0)))
    lat = scale * jnp.concatenate([y[:, :-1], jnp.zeros((full, 1), f32)], 1)
    ends = ((PAD, length - PAD - full), (0, 0))
    diag, lon, lat = (jnp.pad(a, ends) for a in (diag, scale * x, lat))
    b = jnp.pad(b, (ends[0], (0, 0), (0, 0))).reshape(length * times, rows)
    c = weights(times)
    c_rows = jnp.broadcast_to(jnp.asarray(c.reshape(-1, 1), f32), ((SWEEPS + 1) * times, rows))
    slab = pltpu.VMEM((length * times, rows), f32)
    solved = pl.pallas_call(
        lambda *refs: sweep_kernel(full, *refs),
        out_shape=jax.ShapeDtypeStruct((length * times, rows), f32),
        in_specs=[VMEM] * 5,
        out_specs=VMEM,
        scratch_shapes=[slab],
        name="sweeps",
    )(b, diag, lon, lat, c_rows)
    solved = solved.reshape(length, times, rows)[PAD + HALO : PAD + HALO + width]
    field = jnp.einsum("kt,jkr->jtr", basis, solved, precision=lax.Precision.HIGHEST)
    field = field.reshape(width, tm, tl, lats, rl).transpose(1, 3, 2, 4, 0).reshape(tm * lats, tl, rl, width)
    back = lax.all_to_all(field, ("tm", "lat"), 0, 0, tiled=True)
    back = back.reshape(tm, fields, parts, tl, rl, width).transpose(1, 3, 4, 0, 2, 5)
    return back.reshape(fields, tl, rl, nlon)


def per_device(states, mass_term, lat_coupling, lon_coupling):
    fields, tl, rl, nlon = states.shape
    tm, lats = lax.axis_size("tm"), lax.axis_size("lat")
    packed = tl == 1 and tm == SUB and lats == fields and rl * lats == LANES
    packed = packed and nlon % (tm * LANES) == 0 and 2 * HALO * rl == SUB * LANES
    packed = packed and (nlon // tm + 2 * HALO) % (LANES // tm) == 0 and tm % PACK_BANDS == 0
    plan = solve_packed if packed else solve_general
    return plan(states, mass_term, lat_coupling, lon_coupling)


def solution(mesh):
    placed = (P(None, "tm", "lat", None), P("lat", None), P("lat", None), P("lat", None))
    return jax.shard_map(
        per_device,
        mesh=mesh,
        in_specs=placed,
        out_specs=P(None, "tm", "lat", None),
        check_vma=False,
    )
```

```python
import math

import jax
import jax.numpy as jnp
import numpy as np
from jax import lax
from jax.experimental import pallas as pl
from jax.experimental.pallas import tpu as pltpu
from jax.sharding import PartitionSpec as P

SWEEPS = 16
HALO = SWEEPS
BAND_TURNS = (0, 2, 4, 6, 1, 3, 5, 7)
PAD = 8
LANES = 128
SUB = 8

mass_low = 0.005
mass_high = 0.05
coupling_high = 2.0
base_shift = 0.002
time_coupling = 0.05
CENTER = (mass_low + mass_high + 8.0 * coupling_high) / 2.0
DELTA = (mass_high + 8.0 * coupling_high - mass_low) / 2.0


def frequencies(times):
    index = np.arange(times)
    return np.where(index <= times // 2, index, index - times // 2).astype(np.float64)


def time_basis(times):
    freq = frequencies(times)
    index = np.arange(times)
    angle = 2.0 * np.pi * freq[:, None] * np.arange(times)[None, :] / times
    edge = ((index == 0) | (index == times // 2))[:, None]
    cosine = np.cos(angle) * np.where(edge, math.sqrt(1.0 / times), math.sqrt(2.0 / times))
    sine = np.sin(angle) * math.sqrt(2.0 / times)
    return np.where((index > times // 2)[:, None], sine, cosine)


def weights(times):
    shift = base_shift + time_coupling * (2.0 - 2.0 * np.cos(2.0 * np.pi * frequencies(times) / times))
    sigma = (shift + CENTER) / DELTA
    second = [np.ones_like(sigma), 2.0 * sigma]
    first = [np.ones_like(sigma), sigma]
    for _ in range(SWEEPS):
        second.append(2.0 * sigma * second[-1] - second[-2])
        first.append(2.0 * sigma * first[-1] - first[-2])
    rows = [2.0 * second[SWEEPS - j] / (DELTA * first[SWEEPS + 1]) for j in range(SWEEPS + 1)]
    return 0.5 * np.stack(rows)


def padded_length(width):
    return -(-(PAD + width + 1) // SUB) * SUB


def run_sweeps(columns, rows, b_ref, p_ref, q_ref, diag_ref, lon_ref, lat_ref, c_ref):
    stride = rows + PAD
    turn = SUB

    def sweep(c, new_ref, old_ref, place_ref, last=False, gain=None):
        for block in range(rows // SUB):

            def at(ref, column, shift=0):
                lo = column * stride + PAD + block * SUB + shift
                return ref[lo : lo + SUB, :]

            def coef(ref, column):
                lo = column * rows + block * SUB
                return ref[lo : lo + SUB, :]

            final = columns - 1
            for n in range(columns):
                near = at(new_ref, n)
                east = at(new_ref, n + 1) if n < final else pltpu.roll(at(new_ref, 0), LANES - turn, 1)
                west = at(new_ref, n - 1) if n > 0 else pltpu.roll(at(new_ref, final), turn, 1)
                lon_west = coef(lon_ref, n - 1) if n > 0 else pltpu.roll(coef(lon_ref, final), turn, 1)
                image = (coef(diag_ref, n) * near + coef(lon_ref, n) * east) + lon_west * west
                image = image + at(lat_ref, n) * at(new_ref, n, 1) + at(lat_ref, n, -1) * at(new_ref, n, -1)
                if gain is not None:
                    image = gain * image
                total = c * at(b_ref, n) + image
                if old_ref is not None:
                    total = total - at(old_ref, n)
                if last:
                    total = total - at(old_ref, n)
                lo = n * stride + PAD + block * SUB
                place_ref[lo : lo + SUB, :] = total

    def wide(degree):
        return jnp.broadcast_to(c_ref[pl.ds(degree, 1), :], (SUB, LANES))

    top = wide(SWEEPS)
    sweep(wide(SWEEPS - 1), b_ref, None, q_ref, gain=top)
    sweep(wide(SWEEPS - 2) - top, q_ref, None, p_ref)

    def pair(index, carry):
        sweep(wide(SWEEPS - 3 - 2 * index), p_ref, q_ref, q_ref)
        sweep(wide(SWEEPS - 4 - 2 * index), q_ref, p_ref, p_ref)
        return carry

    lax.fori_loop(0, SWEEPS // 2 - 2, pair, 0)
    sweep(wide(1), p_ref, q_ref, q_ref)
    sweep(wide(0), q_ref, p_ref, p_ref, last=True)


R2 = math.sqrt(0.5)


def spread(x):
    e1, e2, e3 = x[1] + x[7], x[2] + x[6], x[3] + x[5]
    o1, o2, o3 = x[1] - x[7], x[2] - x[6], x[3] - x[5]
    a, b = x[0] + x[4], x[0] - x[4]
    p, m, q, n = e1 + e3, R2 * (e1 - e3), a + e2, R2 * (o1 + o3)
    return [q + p, b + m, a - e2, b - m, q - p, n + o2, o1 - o3, n - o2]


def gather_times(v):
    s, d = v[0] + v[4], v[0] - v[4]
    m, p, n = R2 * (v[1] - v[3]), v[1] + v[3], R2 * (v[5] + v[7])
    sv, g, h = s + v[2], s - v[2], v[5] - v[7]
    dp, dm, np_, nm = d + m, d - m, n + v[6], n - v[6]
    return [sv + p, dp + np_, g + h, dm + nm, sv - p, dm - nm, g - h, dp - np_]


def halo_group(pieces, width):
    lane = lax.broadcasted_iota(jnp.int32, (SUB, LANES), 1)
    groups = LANES // width
    out = []
    for q in range(groups):
        tile = None
        for g, piece in enumerate(pieces):
            moved = piece if g == q else pltpu.roll(piece, (width * (g - q)) % LANES, 1)
            tile = moved if tile is None else jnp.where(lane < width * g, tile, moved)
        out.append(tile)
    return out


def pack_halo(west, east):
    rl = west.shape[0]
    lane = lax.broadcasted_iota(jnp.int32, (rl, LANES), 1)
    small = lax.broadcasted_iota(jnp.int32, (SUB, LANES), 1)
    both = pltpu.roll(jnp.where(lane < LANES // 2, east, west), HALO, 1)
    tile = None
    for q in range(rl // SUB):
        piece = both[q * SUB : (q + 1) * SUB]
        moved = piece if q == 0 else pltpu.roll(piece, 2 * HALO * q, 1)
        tile = moved if tile is None else jnp.where(small < 2 * HALO * q, tile, moved)
    return tile


def relative(place, turn):
    return lax.bitwise_xor(place, jnp.int32(turn))


def pack_kernel(here_ref, s_ref, *refs):
    coef_refs, early_ref, late_refs = refs[:3], refs[3], refs[4:8]
    s_v, e_v, l_v, west_v, near_v, east_v, c_v, s_sem, c_sem, e_sem, l_sem = refs[8:]
    rl, total = s_ref.shape[1:]
    width = 2 * LANES
    bands = total // width
    lane = lax.broadcasted_iota(jnp.int32, (rl, LANES), 1)
    order = [1, 2, 3, 0]
    loads = {r: pltpu.make_async_copy(s_ref.at[relative(here_ref[1], r)], s_v.at[r], s_sem.at[r]) for r in order}
    band = here_ref[0]
    starts = [lax.rem(band * width + (total - LANES), total), band * width, lax.rem((band + 1) * width, total)]
    starts = [pl.multiple_of(start, LANES) for start in starts]
    pieces = []
    for n, ref in enumerate(coef_refs):
        for k, (start, v) in enumerate(zip(starts, (west_v, near_v, east_v))):
            part = ref.at[:, pl.ds(start, v.shape[2])]
            pieces.append(pltpu.make_async_copy(part, v.at[n], c_sem.at[n * 3 + k]))
    loads[order[0]].start()
    for piece in pieces:
        piece.start()
    for r in order[1:]:
        loads[r].start()
    for place, r in enumerate(order):
        loads[r].wait()
        for i in range(bands):
            lo = i * width
            west = (lo - LANES) % total
            after = (lo + width) % total
            near, far = s_v[r, :, lo : lo + LANES], s_v[r, :, lo + LANES : lo + width]
            e_v[r, i, :rl, :] = near
            e_v[r, i, rl:, :] = pack_halo(s_v[r, :, west : west + LANES], far)
            turn = relative(here_ref[0], i)
            row = ((turn & 1) * (bands // 2) + lax.shift_right_logical(turn, 1)) * rl
            both = jnp.where(lane < HALO, s_v[r, :, after : after + LANES], far)
            l_v[r, pl.ds(pl.multiple_of(row, SUB), rl), :] = pltpu.roll(both, LANES - HALO, 1)
        pltpu.make_async_copy(l_v.at[r], late_refs[r].at[: bands * rl], l_sem.at[r]).start()
        pltpu.make_async_copy(e_v.at[r], early_ref.at[:, relative(here_ref[1], r)], e_sem.at[r]).start()
        if place == 0:
            for piece in pieces:
                piece.wait()
            height = c_v.shape[0] // 3
            for n in range(3):
                lo = n * height
                for h in range(2):
                    c_v[lo + h * rl : lo + (h + 1) * rl, :] = near_v[n, :, h * LANES : (h + 1) * LANES]
                c_v[lo + 2 * rl : lo + height, :] = pack_halo(west_v[n], east_v[n])
            for r2 in order:
                pltpu.make_async_copy(c_v, late_refs[r2].at[bands * rl :], l_sem.at[len(order) + r2]).start()
    for r in order:
        pltpu.make_async_copy(l_v.at[r], late_refs[r].at[: bands * rl], l_sem.at[r]).wait()
        pltpu.make_async_copy(e_v.at[r], early_ref.at[:, relative(here_ref[1], r)], e_sem.at[r]).wait()
        pltpu.make_async_copy(c_v, late_refs[r].at[bands * rl :], l_sem.at[len(order) + r]).wait()


def unpack_kernel(here_ref, g_ref, *refs):
    out_ref = refs[-1]
    fields, _, total = out_ref.shape
    width = 2 * LANES
    for i in range(total // width):
        band = relative(here_ref[0], BAND_TURNS[i])
        lo = pl.multiple_of(band * width, LANES)
        for f in range(fields):
            out_ref[f, :, i * width + LANES : (i + 1) * width] = g_ref[i * fields + f]
            out_ref[relative(here_ref[1], f), :, pl.ds(lo, LANES)] = refs[f][i]


def moving(plan):
    def kernel(ins, outs, *refs):
        for target, at, source, of in plan:
            refs[ins + target][at] = refs[source][of]

    return kernel


def shuffle(plan, arrays, shapes):
    kernel = moving(plan)
    count = len(arrays)
    size = sum(math.prod(shape) for shape in shapes)
    return pl.pallas_call(
        lambda *refs: kernel(count, len(shapes), *refs),
        out_shape=tuple(jax.ShapeDtypeStruct(shape, jnp.float32) for shape in shapes),
        in_specs=[VMEM] * count,
        out_specs=(VMEM,) * len(shapes),
        cost_estimate=pl.CostEstimate(flops=0, transcendentals=0, bytes_accessed=8 * size),
        compiler_params=params(16 << 20),
    )(*arrays)


def finish_coefficients(m, y, x):
    scale = 2.0 / DELTA
    lane = lax.broadcasted_iota(jnp.int32, m.shape, 1)
    south = jnp.where(lane == 0, 0.0, pltpu.roll(y, 1, 1))
    west = pltpu.roll(x, 1, 0)
    diag = scale * (CENTER - m - (y + south) - (x + west))
    return diag, scale * x, scale * y


def coef_kernel(first, here_ref, g0, g1, g2, g3, diag_ref, lon_ref, lat_ref, t_ref, tile_ref):
    count, full, rows = t_ref.shape
    width = full - 2 * HALO
    received = (g0, g1, g2, g3)
    rl = rows // len(received)
    height = full * rl // LANES
    tiles = width // LANES

    def block(r, shift=0):
        return pl.multiple_of(relative(here_ref[1], r) * rl + shift, SUB)

    for n in range(count):
        for h in range(tiles):
            for r, g_ref in enumerate(received):
                lo = first + n * height + h * rl
                tile_ref[pl.ds(block(r), rl), :] = g_ref[lo : lo + rl, :]
            t_ref[n, HALO + h * LANES : HALO + (h + 1) * LANES, :] = tile_ref[...].T
    for r, g_ref in enumerate(received):
        lows = [first + n * height + tiles * rl for n in range(count)]
        got = halo_group([g_ref[lo : lo + SUB, :] for lo in lows], 2 * HALO)
        for q, piece in enumerate(got):
            tile_ref[pl.ds(block(r, q * SUB), SUB), :] = piece
    turned = tile_ref[...].T
    for n in range(count):
        t_ref[n, :HALO, :] = turned[n * 2 * HALO : n * 2 * HALO + HALO]
        t_ref[n, HALO + width :, :] = turned[n * 2 * HALO + HALO : (n + 1) * 2 * HALO]
    for ref, value in zip((diag_ref, lon_ref, lat_ref), finish_coefficients(t_ref[0], t_ref[1], t_ref[2])):
        ref[...] = value


def solve_columns(first, coefs, c_ref, p_ref, work, line_ref):
    b_ref, q_ref, diag_ref, lon_ref, lat_ref = work
    rows = line_ref.shape[1]
    times = SUB
    groups = LANES // times
    columns = line_ref.shape[0] // LANES
    stride = rows + PAD
    zero = jnp.zeros((PAD, LANES), jnp.float32)
    for ref in (b_ref, p_ref, q_ref, lat_ref):
        for c in range(columns + 1):
            ref[c * stride : c * stride + PAD, :] = zero

    def place(group, column):
        lo = (group * columns + column) * times
        return slice(lo, lo + times)

    for c in range(columns):
        for ref, out_ref in zip(coefs, (diag_ref, lon_ref, lat_ref)):
            picked = [ref[first + g * columns + c : first + g * columns + c + 1, :] for g in range(groups)]
            turned = jnp.concatenate([jnp.broadcast_to(row, (times, rows)) for row in picked], 0).T
            lo = c * stride + PAD if out_ref is lat_ref else c * rows
            out_ref[lo : lo + rows, :] = turned
        turned = jnp.concatenate([line_ref[place(g, c), :] for g in range(groups)], 0).T
        b_ref[c * stride + PAD : (c + 1) * stride, :] = turned
    run_sweeps(columns, rows, b_ref, p_ref, q_ref, diag_ref, lon_ref, lat_ref, c_ref)
    for c in range(columns):
        turned = p_ref[c * stride + PAD : (c + 1) * stride, :].T
        for g in range(groups):
            line_ref[place(g, c), :] = turned[g * times : (g + 1) * times]


def to_frequencies(t_ref, line_ref, first):
    times = t_ref.shape[0]

    def step(block, carry):
        lo = pl.multiple_of(block * SUB, SUB)
        v = spread([t_ref[t, pl.ds(lo, SUB), :] for t in range(times)])
        for k in range(times):
            line_ref[pl.ds(lo * times + k, SUB, stride=times), :] = v[k]
        return carry

    lax.fori_loop(first // SUB, t_ref.shape[1] // SUB, step, 0)


def to_times(line_ref, t_ref):
    times = t_ref.shape[0]

    def step(block, carry):
        lo = pl.multiple_of(block * SUB, SUB)
        base = (HALO + lo) * times
        v = gather_times([line_ref[pl.ds(base + k, SUB, stride=times), :] for k in range(times)])
        for t in range(times):
            t_ref[t, pl.ds(lo, SUB), :] = v[t]
        return carry

    lax.fori_loop(0, LANES // SUB, step, 0)


def solve_early_kernel(here_ref, g_ref, diag_ref, lon_ref, lat_ref, c_ref, z0, z1, z2, z3, keep_ref, t_ref, line_ref, tile_ref, p_ref, *work):
    times, _, rows = t_ref.shape
    lats = g_ref.shape[0] // times
    rl = rows // lats
    for t in range(times):
        turned = jnp.concatenate([g_ref[t * lats + l, :rl, :] for l in range(lats)], 0).T
        t_ref[t, HALO : HALO + LANES, :] = turned
    per = LANES // (2 * HALO)
    for g in range(times // per):
        for l in range(lats):
            got = halo_group([g_ref[(g * per + n) * lats + l, rl:, :] for n in range(per)], 2 * HALO)
            for q, piece in enumerate(got):
                tile_ref[l * rl + q * SUB : l * rl + (q + 1) * SUB, :] = piece
        turned = tile_ref[...].T
        for n in range(per):
            t_ref[g * per + n, :HALO, :] = turned[n * 2 * HALO : n * 2 * HALO + HALO]
            t_ref[g * per + n, HALO + LANES :, :] = turned[n * 2 * HALO + HALO : (n + 1) * 2 * HALO]
    to_frequencies(t_ref, line_ref, 0)
    keep_ref[...] = line_ref[LANES * times :, :]
    solve_columns(0, (diag_ref, lon_ref, lat_ref), c_ref, p_ref, work, line_ref)
    to_times(line_ref, t_ref)
    for q, ref in enumerate((z0, z1, z2, z3)):
        for p in range(2):
            tile_ref[...] = t_ref[relative(here_ref[0], 2 * q + p), :LANES, :].T
            for r in range(lats):
                lo = pl.multiple_of(relative(here_ref[1], r) * rl, SUB)
                ref[p, r] = tile_ref[pl.ds(lo, rl), :]


def solve_late_kernel(here_ref, z0, z1, z2, z3, keep_ref, diag_ref, lon_ref, lat_ref, c_ref, out_ref, t_ref, line_ref, tile_ref, p_ref, *work):
    times, _, rows = t_ref.shape
    lats = out_ref.shape[0] // times
    rl = rows // lats
    for q, ref in enumerate((z0, z1, z2, z3)):
        for p in range(2):
            for r in range(lats):
                lo = pl.multiple_of(relative(here_ref[1], r) * rl, SUB)
                tile_ref[pl.ds(lo, rl), :] = ref[p, r]
            t_ref[relative(here_ref[0], 2 * q + p), 2 * HALO :, :] = tile_ref[...].T
    line_ref[: 2 * HALO * times, :] = keep_ref[...]
    to_frequencies(t_ref, line_ref, 2 * HALO)
    solve_columns(LANES, (diag_ref, lon_ref, lat_ref), c_ref, p_ref, work, line_ref)
    to_times(line_ref, t_ref)
    for t in range(times):
        turned = t_ref[t, :LANES, :].T
        for l in range(lats):
            out_ref[t * lats + l] = turned[l * rl : (l + 1) * rl]


def sweep_kernel(width, b_ref, diag_ref, lon_ref, lat_ref, c_ref, p_ref, q_ref):
    times = c_ref.shape[0] // (SWEEPS + 1)
    lanes = b_ref.shape[1]

    def rows(j):
        return pl.ds(pl.multiple_of(j * times, SUB), times)

    def wide(ref, j):
        return jnp.broadcast_to(ref[pl.ds(j, 1), :], (times, lanes))

    def begin(j, carry):
        p_ref[rows(j), :] = c_ref[SWEEPS * times :, :] * b_ref[rows(j), :]
        q_ref[rows(j), :] = jnp.zeros((times, lanes), jnp.float32)
        return carry

    lax.fori_loop(0, b_ref.shape[0] // times, begin, 0)

    def sweep(degree, new_ref, old_ref, last=False):
        def step(j, carry):
            j = j + PAD
            near = new_ref[rows(j), :]
            image = wide(diag_ref, j) * near + wide(lon_ref, j) * new_ref[rows(j + 1), :]
            image = image + wide(lon_ref, j - 1) * new_ref[rows(j - 1), :]
            lat = wide(lat_ref, j)
            image = image + lat * pltpu.roll(near, lanes - 1, 1) + pltpu.roll(lat * near, 1, 1)
            older = old_ref[rows(j), :]
            total = c_ref[rows(degree), :] * b_ref[rows(j), :] + image - older
            old_ref[rows(j), :] = total - older if last else total
            return carry

        lax.fori_loop(0, width, step, 0)

    def pair(index, carry):
        sweep(SWEEPS - 1 - 2 * index, p_ref, q_ref)
        sweep(SWEEPS - 2 - 2 * index, q_ref, p_ref)
        return carry

    lax.fori_loop(0, SWEEPS // 2 - 1, pair, 0)
    sweep(1, p_ref, q_ref)
    sweep(0, q_ref, p_ref, True)


VMEM = pl.BlockSpec(memory_space=pltpu.VMEM)
SMEM = pl.BlockSpec(memory_space=pltpu.SMEM)


PACK_PARAMS = pltpu.CompilerParams(vmem_limit_bytes=63 << 20)


def params(limit=None):
    return pltpu.CompilerParams(vmem_limit_bytes=limit)


def called(kernel, **settings):
    return pl.pallas_call(kernel, **settings)


def solve_packed(states, mass_term, lat_coupling, lon_coupling):
    fields, _, rl, nlon = states.shape
    times, lats = lax.axis_size("tm"), lax.axis_size("lat")
    width = nlon // times
    rows = rl * lats
    full = width + 2 * HALO
    height = full * rl // LANES
    f32 = jnp.float32
    part = LANES + 2 * HALO
    fast = params(16 << 20)

    def shaped(*shape):
        return jax.ShapeDtypeStruct(shape, f32)

    def cost(size, flops=0):
        return pl.CostEstimate(flops=flops, transcendentals=0, bytes_accessed=8 * size)

    def swap(array, axis, turn):
        count = lax.axis_size(axis)
        return lax.ppermute(array, axis, [(n, n ^ turn) for n in range(count)])

    here = jnp.stack([lax.axis_index("tm"), lax.axis_index("lat")]).astype(jnp.int32)
    local = states.reshape(fields, rl, nlon)
    edge = part * rl // LANES
    held = times * rl
    dma = pltpu.SemaphoreType.DMA
    HBM = pl.BlockSpec(memory_space=pltpu.MemorySpace.HBM)
    early, *late = pl.pallas_call(
        pack_kernel,
        out_shape=(shaped(times, fields, edge, LANES),) + (shaped(held + 3 * height, LANES),) * lats,
        in_specs=[SMEM] + [HBM] * 4,
        out_specs=(HBM,) * (lats + 1),
        scratch_shapes=[
            pltpu.VMEM((fields, rl, nlon), f32),
            pltpu.VMEM((fields, times, edge, LANES), f32),
            pltpu.VMEM((lats, held, LANES), f32),
            pltpu.VMEM((3, rl, LANES), f32),
            pltpu.VMEM((3, rl, width), f32),
            pltpu.VMEM((3, rl, LANES), f32),
            pltpu.VMEM((3 * height, LANES), f32),
            dma((fields,)),
            dma((9,)),
            dma((fields,)),
            dma((2 * lats,)),
        ],
        cost_estimate=cost(states.size),
        compiler_params=PACK_PARAMS,
        name="pack",
    )(here, local, mass_term, lat_coupling, lon_coupling)
    late = [late[0]] + [swap(late[r], "lat", r) for r in range(1, lats)]
    early = lax.all_to_all(early.reshape(times * lats, edge, LANES), ("tm", "lat"), 0, 0, tiled=True)
    coefs = pl.pallas_call(
        lambda *refs: coef_kernel(held, *refs),
        out_shape=(shaped(full, rows),) * 3,
        in_specs=[SMEM] + [VMEM] * lats,
        out_specs=(VMEM,) * 3,
        scratch_shapes=[pltpu.VMEM((3, full, rows), f32), pltpu.VMEM((rows, LANES), f32)],
        cost_estimate=cost(6 * full * rows, 30 * full * rows),
        compiler_params=fast,
        name="coefficients",
    )(here, *late)

    zs = times // 2
    block = (rl, LANES)

    def of(p, q):
        return slice((p * zs + q) * rl, (p * zs + q + 1) * rl)

    plan = [(0, (r, q), r, of(1, q)) for r in range(lats) for q in range(zs)]
    other = shuffle(plan, late, [(lats, zs) + block])[0]
    other = swap(other, "tm", 1)
    plan = [(q, (0, r), r, of(0, q)) for r in range(lats) for q in range(zs)]
    plan += [(q, (1, r), lats, (r, q)) for r in range(lats) for q in range(zs)]
    inward = shuffle(plan, late + [other], [(2, lats) + block] * zs)
    inward = [inward[0]] + [swap(inward[q], "tm", 2 * q) for q in range(1, zs)]

    groups = LANES // times
    columns = part // groups
    slab = pltpu.VMEM(((rows + PAD) * columns + PAD, LANES), f32)
    flat = pltpu.VMEM((rows * columns, LANES), f32)
    scratch = [pltpu.VMEM((times, part, rows), f32), pltpu.VMEM((part * times, rows), f32), pltpu.VMEM((rows, LANES), f32)]
    scratch += [slab, slab, slab, flat, flat, slab]
    basis = time_basis(times)
    scale = np.max(np.abs(basis), 1) ** 2
    scale = np.where(scale > 1.5 / times, 2.0 / times, 1.0 / times)
    c_rows = jnp.asarray(np.tile(weights(times) * scale[None, :], (1, groups)), f32)
    work = cost(part * times * rows, 16 * SWEEPS * part * times * rows)
    *outward, keep = called(
        solve_early_kernel,
        out_shape=(shaped(2, lats, *block),) * zs + (shaped(2 * HALO * times, rows),),
        in_specs=[SMEM] + [VMEM] * 5,
        out_specs=(VMEM,) * (zs + 1),
        scratch_shapes=scratch,
        cost_estimate=work,
        compiler_params=params(24 << 20),
        name="solve_early",
    )(here, early, *coefs, c_rows)
    outward = [outward[0]] + [swap(outward[q], "tm", 2 * q) for q in range(1, zs)]
    out = called(
        solve_late_kernel,
        out_shape=shaped(times * lats, *block),
        in_specs=[SMEM] + [VMEM] * (zs + 5),
        out_specs=VMEM,
        scratch_shapes=scratch,
        cost_estimate=work,
        compiler_params=params(24 << 20),
        name="solve_late",
    )(here, *inward, keep, *coefs, c_rows)
    back = lax.all_to_all(out, ("tm", "lat"), 0, 0, tiled=True)

    plan = [(0, (q, r), q, (1, r)) for r in range(lats) for q in range(zs)]
    other = shuffle(plan, outward, [(zs, lats) + block])[0]
    other = swap(other, "tm", 1)
    plan = [(r, q, q, (0, r)) for r in range(lats) for q in range(zs)]
    plan += [(r, zs + q, zs, (q, r)) for r in range(lats) for q in range(zs)]
    home = shuffle(plan, outward + [other], [(times,) + block] * lats)
    home = [home[0]] + [swap(home[r], "lat", r) for r in range(1, lats)]
    result = pl.pallas_call(
        unpack_kernel,
        out_shape=shaped(fields, rl, nlon),
        in_specs=[SMEM] + [VMEM] * (lats + 1),
        out_specs=VMEM,
        cost_estimate=cost(states.size),
        compiler_params=fast,
        name="unpack",
    )(here, back, *home)
    return result.reshape(states.shape)


def solve_general(states, mass_term, lat_coupling, lon_coupling):
    fields, tl, rl, nlon = states.shape
    tm, lats = lax.axis_size("tm"), lax.axis_size("lat")
    times, rows, parts = tl * tm, rl * lats, lats // fields
    width = nlon // (tm * parts)
    full = width + 2 * HALO
    length = padded_length(full)
    f32 = jnp.float32

    def wrapped(a):
        return jnp.concatenate([a[..., nlon - HALO :], a, a[..., :HALO]], -1)

    wide = wrapped(states)
    bands = jnp.stack([wide[..., n * width : n * width + full] for n in range(tm * parts)])
    bands = bands.reshape(tm, parts, fields, tl, rl, full).transpose(0, 2, 1, 3, 4, 5)
    got = lax.all_to_all(bands.reshape(tm * lats, tl, rl, full), ("tm", "lat"), 0, 0, tiled=True)
    field = got.reshape(tm, lats, tl, rl, full).transpose(4, 0, 2, 1, 3).reshape(full, times, rows)
    basis = jnp.asarray(time_basis(times), f32)
    b = jnp.einsum("kt,jtr->jkr", basis, field, precision=lax.Precision.HIGHEST)
    coef = wrapped(jnp.stack([mass_term, lat_coupling, lon_coupling]))
    first = lax.axis_index("tm") * parts
    mine = jnp.stack([lax.dynamic_slice_in_dim(coef, (first + n) * width, full, 2) for n in range(parts)])
    mine = jnp.broadcast_to(mine[None], (fields,) + mine.shape).reshape(lats, 3, rl, full)
    all_rows = lax.all_to_all(mine, "lat", 0, 0, tiled=True)
    m, y, x = all_rows.transpose(1, 3, 0, 2).reshape(3, full, rows)
    scale = 2.0 / DELTA
    south = jnp.concatenate([jnp.zeros((full, 1), f32), y[:, :-1]], 1)
    diag = scale * (CENTER - m - (y + south) - (x + jnp.roll(x, 1, 0)))
    lat = scale * jnp.concatenate([y[:, :-1], jnp.zeros((full, 1), f32)], 1)
    ends = ((PAD, length - PAD - full), (0, 0))
    diag, lon, lat = (jnp.pad(a, ends) for a in (diag, scale * x, lat))
    b = jnp.pad(b, (ends[0], (0, 0), (0, 0))).reshape(length * times, rows)
    c = weights(times)
    c_rows = jnp.broadcast_to(jnp.asarray(c.reshape(-1, 1), f32), ((SWEEPS + 1) * times, rows))
    slab = pltpu.VMEM((length * times, rows), f32)
    solved = pl.pallas_call(
        lambda *refs: sweep_kernel(full, *refs),
        out_shape=jax.ShapeDtypeStruct((length * times, rows), f32),
        in_specs=[VMEM] * 5,
        out_specs=VMEM,
        scratch_shapes=[slab],
        name="sweeps",
    )(b, diag, lon, lat, c_rows)
    solved = solved.reshape(length, times, rows)[PAD + HALO : PAD + HALO + width]
    field = jnp.einsum("kt,jkr->jtr", basis, solved, precision=lax.Precision.HIGHEST)
    field = field.reshape(width, tm, tl, lats, rl).transpose(1, 3, 2, 4, 0).reshape(tm * lats, tl, rl, width)
    back = lax.all_to_all(field, ("tm", "lat"), 0, 0, tiled=True)
    back = back.reshape(tm, fields, parts, tl, rl, width).transpose(1, 3, 4, 0, 2, 5)
    return back.reshape(fields, tl, rl, nlon)


def per_device(states, mass_term, lat_coupling, lon_coupling):
    fields, tl, rl, nlon = states.shape
    tm, lats = lax.axis_size("tm"), lax.axis_size("lat")
    packed = tl == 1 and tm == SUB and lats == fields == 4 and rl * lats == LANES
    packed = packed and nlon == 2 * tm * LANES and 2 * HALO * rl == SUB * LANES
    plan = solve_packed if packed else solve_general
    return plan(states, mass_term, lat_coupling, lon_coupling)


def solution(mesh):
    placed = (P(None, "tm", "lat", None), P("lat", None), P("lat", None), P("lat", None))
    return jax.shard_map(
        per_device,
        mesh=mesh,
        in_specs=placed,
        out_specs=P(None, "tm", "lat", None),
        check_vma=False,
    )
```

```python
import math

import jax
import jax.numpy as jnp
import numpy as np
from jax import lax
from jax.experimental import pallas as pl
from jax.experimental.pallas import tpu as pltpu
from jax.sharding import PartitionSpec as P

SWEEPS = 16
HALO = SWEEPS
BAND_TURNS = (0, 2, 4, 6, 1, 3, 5, 7)
ROW_BITS = 2
PAD = 8
LANES = 128
SUB = 8

mass_low = 0.005
mass_high = 0.05
coupling_high = 2.0
base_shift = 0.002
time_coupling = 0.05
CENTER = (mass_low + mass_high + 8.0 * coupling_high) / 2.0
DELTA = (mass_high + 8.0 * coupling_high - mass_low) / 2.0


def frequencies(times):
    index = np.arange(times)
    return np.where(index <= times // 2, index, index - times // 2).astype(np.float64)


def time_basis(times):
    freq = frequencies(times)
    index = np.arange(times)
    angle = 2.0 * np.pi * freq[:, None] * np.arange(times)[None, :] / times
    edge = ((index == 0) | (index == times // 2))[:, None]
    cosine = np.cos(angle) * np.where(edge, math.sqrt(1.0 / times), math.sqrt(2.0 / times))
    sine = np.sin(angle) * math.sqrt(2.0 / times)
    return np.where((index > times // 2)[:, None], sine, cosine)


def weights(times):
    shift = base_shift + time_coupling * (2.0 - 2.0 * np.cos(2.0 * np.pi * frequencies(times) / times))
    sigma = (shift + CENTER) / DELTA
    second = [np.ones_like(sigma), 2.0 * sigma]
    first = [np.ones_like(sigma), sigma]
    for _ in range(SWEEPS):
        second.append(2.0 * sigma * second[-1] - second[-2])
        first.append(2.0 * sigma * first[-1] - first[-2])
    rows = [2.0 * second[SWEEPS - j] / (DELTA * first[SWEEPS + 1]) for j in range(SWEEPS + 1)]
    return 0.5 * np.stack(rows)


def padded_length(width):
    return -(-(PAD + width + 1) // SUB) * SUB


def run_sweeps(columns, rows, b_ref, p_ref, q_ref, diag_ref, lon_ref, lat_ref, c_ref):
    stride = rows + PAD
    turn = SUB

    def sweep(c, new_ref, old_ref, place_ref, last=False, gain=None):
        for block in range(rows // SUB):

            def at(ref, column, shift=0):
                lo = column * stride + PAD + block * SUB + shift
                return ref[lo : lo + SUB, :]

            def coef(ref, column):
                lo = column * rows + block * SUB
                return ref[lo : lo + SUB, :]

            final = columns - 1
            for n in range(columns):
                near = at(new_ref, n)
                east = at(new_ref, n + 1) if n < final else pltpu.roll(at(new_ref, 0), LANES - turn, 1)
                west = at(new_ref, n - 1) if n > 0 else pltpu.roll(at(new_ref, final), turn, 1)
                lon_west = coef(lon_ref, n - 1) if n > 0 else pltpu.roll(coef(lon_ref, final), turn, 1)
                image = (coef(diag_ref, n) * near + coef(lon_ref, n) * east) + lon_west * west
                image = image + at(lat_ref, n) * at(new_ref, n, 1) + at(lat_ref, n, -1) * at(new_ref, n, -1)
                if gain is not None:
                    image = gain * image
                total = c * at(b_ref, n) + image
                if old_ref is not None:
                    total = total - at(old_ref, n)
                if last:
                    total = total - at(old_ref, n)
                lo = n * stride + PAD + block * SUB
                place_ref[lo : lo + SUB, :] = total

    def wide(degree):
        return jnp.broadcast_to(c_ref[pl.ds(degree, 1), :], (SUB, LANES))

    top = wide(SWEEPS)
    sweep(wide(SWEEPS - 1), b_ref, None, q_ref, gain=top)
    sweep(wide(SWEEPS - 2) - top, q_ref, None, p_ref)

    def pair(index, carry):
        sweep(wide(SWEEPS - 3 - 2 * index), p_ref, q_ref, q_ref)
        sweep(wide(SWEEPS - 4 - 2 * index), q_ref, p_ref, p_ref)
        return carry

    lax.fori_loop(0, SWEEPS // 2 - 2, pair, 0)
    sweep(wide(1), p_ref, q_ref, q_ref)
    sweep(wide(0), q_ref, p_ref, p_ref, last=True)


R2 = math.sqrt(0.5)


def spread(x):
    e1, e2, e3 = x[1] + x[7], x[2] + x[6], x[3] + x[5]
    o1, o2, o3 = x[1] - x[7], x[2] - x[6], x[3] - x[5]
    a, b = x[0] + x[4], x[0] - x[4]
    p, m, q, n = e1 + e3, R2 * (e1 - e3), a + e2, R2 * (o1 + o3)
    return [q + p, b + m, a - e2, b - m, q - p, n + o2, o1 - o3, n - o2]


def gather_times(v):
    s, d = v[0] + v[4], v[0] - v[4]
    m, p, n = R2 * (v[1] - v[3]), v[1] + v[3], R2 * (v[5] + v[7])
    sv, g, h = s + v[2], s - v[2], v[5] - v[7]
    dp, dm, np_, nm = d + m, d - m, n + v[6], n - v[6]
    return [sv + p, dp + np_, g + h, dm + nm, sv - p, dm - nm, g - h, dp - np_]


def halo_group(pieces, width):
    lane = lax.broadcasted_iota(jnp.int32, (SUB, LANES), 1)
    groups = LANES // width
    out = []
    for q in range(groups):
        tile = None
        for g, piece in enumerate(pieces):
            moved = piece if g == q else pltpu.roll(piece, (width * (g - q)) % LANES, 1)
            tile = moved if tile is None else jnp.where(lane < width * g, tile, moved)
        out.append(tile)
    return out


def pack_halo(west, east):
    rl = west.shape[0]
    lane = lax.broadcasted_iota(jnp.int32, (rl, LANES), 1)
    small = lax.broadcasted_iota(jnp.int32, (SUB, LANES), 1)
    both = pltpu.roll(jnp.where(lane < LANES // 2, east, west), HALO, 1)
    tile = None
    for q in range(rl // SUB):
        piece = both[q * SUB : (q + 1) * SUB]
        moved = piece if q == 0 else pltpu.roll(piece, 2 * HALO * q, 1)
        tile = moved if tile is None else jnp.where(small < 2 * HALO * q, tile, moved)
    return tile


def time_place(here_ref):
    return lax.shift_right_logical(here_ref[0], ROW_BITS)


def row_place(here_ref):
    return here_ref[0] & ((1 << ROW_BITS) - 1)


def relative(place, turn):
    return lax.bitwise_xor(place, jnp.int32(turn))


def pack_kernel(here_ref, s_ref, early_ref, l0, l1, l2, l3, s_v, e_v, l_v, s_sem, e_sem, l_sem):
    late_refs = (l0, l1, l2, l3)
    rl, total = s_ref.shape[1:]
    width = 2 * LANES
    bands = total // width
    lane = lax.broadcasted_iota(jnp.int32, (rl, LANES), 1)
    order = [1, 2, 3, 0]
    loads = {r: pltpu.make_async_copy(s_ref.at[relative(row_place(here_ref), r)], s_v.at[r], s_sem.at[r]) for r in order}
    for r in order:
        loads[r].start()
    sent = []
    for r in order:
        loads[r].wait()
        for i in range(bands):
            lo = i * width
            west = (lo - LANES) % total
            after = (lo + width) % total
            near, far = s_v[r, :, lo : lo + LANES], s_v[r, :, lo + LANES : lo + width]
            e_v[r, i, :rl, :] = near
            e_v[r, i, rl:, :] = pack_halo(s_v[r, :, west : west + LANES], far)
            turn = relative(time_place(here_ref), i)
            row = ((turn & 1) * (bands // 2) + lax.shift_right_logical(turn, 1)) * rl
            both = jnp.where(lane < HALO, s_v[r, :, after : after + LANES], far)
            l_v[r, pl.ds(pl.multiple_of(row, SUB), rl), :] = pltpu.roll(both, LANES - HALO, 1)
        sent.append(pltpu.make_async_copy(e_v.at[r], early_ref.at[:, relative(row_place(here_ref), r)], e_sem.at[r]))
        sent[-1].start()
        sent.append(pltpu.make_async_copy(l_v.at[r], late_refs[r], l_sem.at[r]))
        sent[-1].start()
    for copy in sent:
        copy.wait()


def pack_coef_kernel(here_ref, m_ref, y_ref, x_ref, coef_ref, west_v, near_v, east_v, c_v, sem, out_sem):
    rl, total = m_ref.shape
    width = 2 * LANES
    height = coef_ref.shape[0] // 3
    band = time_place(here_ref)
    starts = [lax.rem(band * width + (total - LANES), total), band * width, lax.rem((band + 1) * width, total)]
    pieces = []
    for n, ref in enumerate((m_ref, y_ref, x_ref)):
        for k, (start, v) in enumerate(zip(starts, (west_v, near_v, east_v))):
            part = ref.at[:, pl.ds(pl.multiple_of(start, LANES), v.shape[2])]
            pieces.append(pltpu.make_async_copy(part, v.at[n], sem.at[n * 3 + k]))
    for piece in pieces:
        piece.start()
    for piece in pieces:
        piece.wait()
    for n in range(3):
        first = n * height
        for h in range(2):
            c_v[first + h * rl : first + (h + 1) * rl, :] = near_v[n, :, h * LANES : (h + 1) * LANES]
        c_v[first + 2 * rl : first + height, :] = pack_halo(west_v[n], east_v[n])
    out = pltpu.make_async_copy(c_v, coef_ref, out_sem)
    out.start()
    out.wait()


def unpack_early_kernel(here_ref, g0, g1, g2, g3, out_ref, sem):
    received = (g0, g1, g2, g3)
    bands, _ = g0.shape[:2]
    width = 2 * LANES
    copies = []
    for r, g_ref in enumerate(received):
        for i in range(bands):
            lo = pl.multiple_of(relative(time_place(here_ref), BAND_TURNS[i]) * width, LANES)
            target = out_ref.at[relative(row_place(here_ref), r), :, pl.ds(lo, LANES)]
            copies.append(pltpu.make_async_copy(g_ref.at[i], target, sem.at[r * bands + i]))
    for copy in copies:
        copy.start()
    for copy in copies:
        copy.wait()


def unpack_late_kernel(g_ref, part_ref, out_ref, sem):
    fields, _, total = out_ref.shape
    width = 2 * LANES
    copies = []
    for i in range(total // width):
        for f in range(fields):
            n = i * fields + f
            target = out_ref.at[f, :, i * width + LANES : (i + 1) * width]
            copies.append(pltpu.make_async_copy(g_ref.at[n], target, sem.at[n]))
    for copy in copies:
        copy.start()
    for copy in copies:
        copy.wait()


def moving(plan):
    def kernel(ins, outs, *refs):
        for target, at, source, of in plan:
            refs[ins + target][at] = refs[source][of]

    return kernel


def shuffle(plan, arrays, shapes):
    kernel = moving(plan)
    count = len(arrays)
    size = sum(math.prod(shape) for shape in shapes)
    return pl.pallas_call(
        lambda *refs: kernel(count, len(shapes), *refs),
        out_shape=tuple(jax.ShapeDtypeStruct(shape, jnp.float32) for shape in shapes),
        in_specs=[VMEM] * count,
        out_specs=(VMEM,) * len(shapes),
        cost_estimate=pl.CostEstimate(flops=0, transcendentals=0, bytes_accessed=8 * size),
        compiler_params=params(16 << 20),
    )(*arrays)


def finish_coefficients(m, y, x):
    scale = 2.0 / DELTA
    lane = lax.broadcasted_iota(jnp.int32, m.shape, 1)
    south = jnp.where(lane == 0, 0.0, pltpu.roll(y, 1, 1))
    west = pltpu.roll(x, 1, 0)
    diag = scale * (CENTER - m - (y + south) - (x + west))
    return diag, scale * x, scale * y


def coef_kernel(first, here_ref, g0, g1, g2, g3, diag_ref, lon_ref, lat_ref, t_ref, tile_ref):
    count, full, rows = t_ref.shape
    width = full - 2 * HALO
    received = (g0, g1, g2, g3)
    rl = rows // len(received)
    height = full * rl // LANES
    tiles = width // LANES

    def block(r, shift=0):
        return pl.multiple_of(relative(row_place(here_ref), r) * rl + shift, SUB)

    for n in range(count):
        for h in range(tiles):
            for r, g_ref in enumerate(received):
                lo = first + n * height + h * rl
                tile_ref[pl.ds(block(r), rl), :] = g_ref[lo : lo + rl, :]
            t_ref[n, HALO + h * LANES : HALO + (h + 1) * LANES, :] = tile_ref[...].T
    for r, g_ref in enumerate(received):
        lows = [first + n * height + tiles * rl for n in range(count)]
        got = halo_group([g_ref[lo : lo + SUB, :] for lo in lows], 2 * HALO)
        for q, piece in enumerate(got):
            tile_ref[pl.ds(block(r, q * SUB), SUB), :] = piece
    turned = tile_ref[...].T
    for n in range(count):
        t_ref[n, :HALO, :] = turned[n * 2 * HALO : n * 2 * HALO + HALO]
        t_ref[n, HALO + width :, :] = turned[n * 2 * HALO + HALO : (n + 1) * 2 * HALO]
    for ref, value in zip((diag_ref, lon_ref, lat_ref), finish_coefficients(t_ref[0], t_ref[1], t_ref[2])):
        ref[...] = value


def solve_columns(first, coefs, c_ref, p_ref, work, line_ref):
    b_ref, q_ref, diag_ref, lon_ref, lat_ref = work
    rows = line_ref.shape[1]
    times = SUB
    groups = LANES // times
    columns = line_ref.shape[0] // LANES
    stride = rows + PAD
    zero = jnp.zeros((PAD, LANES), jnp.float32)
    for ref in (b_ref, p_ref, q_ref, lat_ref):
        for c in range(columns + 1):
            ref[c * stride : c * stride + PAD, :] = zero

    def place(group, column):
        lo = (group * columns + column) * times
        return slice(lo, lo + times)

    for c in range(columns):
        for ref, out_ref in zip(coefs, (diag_ref, lon_ref, lat_ref)):
            picked = [ref[first + g * columns + c : first + g * columns + c + 1, :] for g in range(groups)]
            turned = jnp.concatenate([jnp.broadcast_to(row, (times, rows)) for row in picked], 0).T
            lo = c * stride + PAD if out_ref is lat_ref else c * rows
            out_ref[lo : lo + rows, :] = turned
        turned = jnp.concatenate([line_ref[place(g, c), :] for g in range(groups)], 0).T
        b_ref[c * stride + PAD : (c + 1) * stride, :] = turned
    run_sweeps(columns, rows, b_ref, p_ref, q_ref, diag_ref, lon_ref, lat_ref, c_ref)
    for c in range(columns):
        turned = p_ref[c * stride + PAD : (c + 1) * stride, :].T
        for g in range(groups):
            line_ref[place(g, c), :] = turned[g * times : (g + 1) * times]


def to_frequencies(t_ref, line_ref, first):
    times = t_ref.shape[0]

    def step(block, carry):
        lo = pl.multiple_of(block * SUB, SUB)
        v = spread([t_ref[t, pl.ds(lo, SUB), :] for t in range(times)])
        for k in range(times):
            line_ref[pl.ds(lo * times + k, SUB, stride=times), :] = v[k]
        return carry

    lax.fori_loop(first // SUB, t_ref.shape[1] // SUB, step, 0)


def to_times(line_ref, t_ref):
    times = t_ref.shape[0]

    def step(block, carry):
        lo = pl.multiple_of(block * SUB, SUB)
        base = (HALO + lo) * times
        v = gather_times([line_ref[pl.ds(base + k, SUB, stride=times), :] for k in range(times)])
        for t in range(times):
            t_ref[t, pl.ds(lo, SUB), :] = v[t]
        return carry

    lax.fori_loop(0, LANES // SUB, step, 0)


def solve_early_kernel(here_ref, g_ref, diag_ref, lon_ref, lat_ref, c_ref, z0, z1, z2, z3, keep_ref, t_ref, line_ref, tile_ref, p_ref, *work):
    times, _, rows = t_ref.shape
    lats = g_ref.shape[0] // times
    rl = rows // lats
    for t in range(times):
        turned = jnp.concatenate([g_ref[t * lats + l, :rl, :] for l in range(lats)], 0).T
        t_ref[t, HALO : HALO + LANES, :] = turned
    per = LANES // (2 * HALO)
    for g in range(times // per):
        for l in range(lats):
            got = halo_group([g_ref[(g * per + n) * lats + l, rl:, :] for n in range(per)], 2 * HALO)
            for q, piece in enumerate(got):
                tile_ref[l * rl + q * SUB : l * rl + (q + 1) * SUB, :] = piece
        turned = tile_ref[...].T
        for n in range(per):
            t_ref[g * per + n, :HALO, :] = turned[n * 2 * HALO : n * 2 * HALO + HALO]
            t_ref[g * per + n, HALO + LANES :, :] = turned[n * 2 * HALO + HALO : (n + 1) * 2 * HALO]
    to_frequencies(t_ref, line_ref, 0)
    keep_ref[...] = line_ref[LANES * times :, :]
    solve_columns(0, (diag_ref, lon_ref, lat_ref), c_ref, p_ref, work, line_ref)
    to_times(line_ref, t_ref)
    for q, ref in enumerate((z0, z1, z2, z3)):
        for p in range(2):
            tile_ref[...] = t_ref[relative(time_place(here_ref), 2 * q + p), :LANES, :].T
            for r in range(lats):
                lo = pl.multiple_of(relative(row_place(here_ref), r) * rl, SUB)
                ref[p, r] = tile_ref[pl.ds(lo, rl), :]


def solve_late_kernel(here_ref, z0, z1, z2, z3, keep_ref, diag_ref, lon_ref, lat_ref, c_ref, out_ref, t_ref, line_ref, tile_ref, p_ref, *work):
    times, _, rows = t_ref.shape
    lats = out_ref.shape[0] // times
    rl = rows // lats
    for q, ref in enumerate((z0, z1, z2, z3)):
        for p in range(2):
            for r in range(lats):
                lo = pl.multiple_of(relative(row_place(here_ref), r) * rl, SUB)
                tile_ref[pl.ds(lo, rl), :] = ref[p, r]
            t_ref[relative(time_place(here_ref), 2 * q + p), 2 * HALO :, :] = tile_ref[...].T
    line_ref[: 2 * HALO * times, :] = keep_ref[...]
    to_frequencies(t_ref, line_ref, 2 * HALO)
    solve_columns(LANES, (diag_ref, lon_ref, lat_ref), c_ref, p_ref, work, line_ref)
    to_times(line_ref, t_ref)
    for t in range(times):
        turned = t_ref[t, :LANES, :].T
        for l in range(lats):
            out_ref[t * lats + l] = turned[l * rl : (l + 1) * rl]


def sweep_kernel(width, b_ref, diag_ref, lon_ref, lat_ref, c_ref, p_ref, q_ref):
    times = c_ref.shape[0] // (SWEEPS + 1)
    lanes = b_ref.shape[1]

    def rows(j):
        return pl.ds(pl.multiple_of(j * times, SUB), times)

    def wide(ref, j):
        return jnp.broadcast_to(ref[pl.ds(j, 1), :], (times, lanes))

    def begin(j, carry):
        p_ref[rows(j), :] = c_ref[SWEEPS * times :, :] * b_ref[rows(j), :]
        q_ref[rows(j), :] = jnp.zeros((times, lanes), jnp.float32)
        return carry

    lax.fori_loop(0, b_ref.shape[0] // times, begin, 0)

    def sweep(degree, new_ref, old_ref, last=False):
        def step(j, carry):
            j = j + PAD
            near = new_ref[rows(j), :]
            image = wide(diag_ref, j) * near + wide(lon_ref, j) * new_ref[rows(j + 1), :]
            image = image + wide(lon_ref, j - 1) * new_ref[rows(j - 1), :]
            lat = wide(lat_ref, j)
            image = image + lat * pltpu.roll(near, lanes - 1, 1) + pltpu.roll(lat * near, 1, 1)
            older = old_ref[rows(j), :]
            total = c_ref[rows(degree), :] * b_ref[rows(j), :] + image - older
            old_ref[rows(j), :] = total - older if last else total
            return carry

        lax.fori_loop(0, width, step, 0)

    def pair(index, carry):
        sweep(SWEEPS - 1 - 2 * index, p_ref, q_ref)
        sweep(SWEEPS - 2 - 2 * index, q_ref, p_ref)
        return carry

    lax.fori_loop(0, SWEEPS // 2 - 1, pair, 0)
    sweep(1, p_ref, q_ref)
    sweep(0, q_ref, p_ref, True)


VMEM = pl.BlockSpec(memory_space=pltpu.VMEM)
SMEM = pl.BlockSpec(memory_space=pltpu.SMEM)


PACK_PARAMS = pltpu.CompilerParams(vmem_limit_bytes=63 << 20)


def params(limit=None):
    return pltpu.CompilerParams(vmem_limit_bytes=limit)


def called(kernel, **settings):
    return pl.pallas_call(kernel, **settings)


def solve_packed(states, mass_term, lat_coupling, lon_coupling):
    fields, _, rl, nlon = states.shape
    times, lats = lax.axis_size("tm"), lax.axis_size("lat")
    width = nlon // times
    rows = rl * lats
    full = width + 2 * HALO
    height = full * rl // LANES
    f32 = jnp.float32
    part = LANES + 2 * HALO
    fast = params(16 << 20)

    def shaped(*shape):
        return jax.ShapeDtypeStruct(shape, f32)

    def cost(size, flops=0):
        return pl.CostEstimate(flops=flops, transcendentals=0, bytes_accessed=8 * size)

    def swap(array, axis, turn):
        count = lax.axis_size(axis)
        return lax.ppermute(array, axis, [(n, n ^ turn) for n in range(count)])

    here = lax.axis_index(("tm", "lat")).astype(jnp.int32).reshape(1)
    local = states.reshape(fields, rl, nlon)
    edge = part * rl // LANES
    held = times * rl
    dma = pltpu.SemaphoreType.DMA
    HBM = pl.BlockSpec(memory_space=pltpu.MemorySpace.HBM)
    early, *late = pl.pallas_call(
        pack_kernel,
        out_shape=(shaped(times, fields, edge, LANES),) + (shaped(held, LANES),) * lats,
        in_specs=[SMEM, HBM],
        out_specs=(HBM,) * (lats + 1),
        scratch_shapes=[
            pltpu.VMEM((fields, rl, nlon), f32),
            pltpu.VMEM((fields, times, edge, LANES), f32),
            pltpu.VMEM((lats, held, LANES), f32),
            dma((fields,)),
            dma((fields,)),
            dma((lats,)),
        ],
        cost_estimate=cost(states.size),
        compiler_params=PACK_PARAMS,
        name="pack",
    )(here, local)
    early = lax.all_to_all(early.reshape(times * lats, edge, LANES), ("tm", "lat"), 0, 0, tiled=True)
    late = [late[0]] + [swap(late[r], "lat", r) for r in range(1, lats)]
    coef = called(
        pack_coef_kernel,
        out_shape=shaped(3 * height, LANES),
        in_specs=[SMEM] + [HBM] * 3,
        out_specs=HBM,
        scratch_shapes=[pltpu.VMEM((3, rl, size), f32) for size in (LANES, width, LANES)]
        + [pltpu.VMEM((3 * height, LANES), f32), dma((9,)), dma(())],
        cost_estimate=cost(2 * mass_term.size),
        compiler_params=PACK_PARAMS,
        name="pack_coefficients",
    )(here, mass_term, lat_coupling, lon_coupling)
    coef = [coef] + [swap(coef, "lat", r) for r in range(1, lats)]
    coefs = pl.pallas_call(
        lambda *refs: coef_kernel(0, *refs),
        out_shape=(shaped(full, rows),) * 3,
        in_specs=[SMEM] + [VMEM] * lats,
        out_specs=(VMEM,) * 3,
        scratch_shapes=[pltpu.VMEM((3, full, rows), f32), pltpu.VMEM((rows, LANES), f32)],
        cost_estimate=cost(6 * full * rows, 30 * full * rows),
        compiler_params=fast,
        name="coefficients",
    )(here, *coef)

    zs = times // 2
    block = (rl, LANES)

    def of(p, q):
        return slice((p * zs + q) * rl, (p * zs + q + 1) * rl)

    plan = [(0, (r, q), r, of(1, q)) for r in range(lats) for q in range(zs)]
    other = shuffle(plan, late, [(lats, zs) + block])[0]
    other = swap(other, "tm", 1)
    plan = [(q, (0, r), r, of(0, q)) for r in range(lats) for q in range(zs)]
    plan += [(q, (1, r), lats, (r, q)) for r in range(lats) for q in range(zs)]
    inward = shuffle(plan, late + [other], [(2, lats) + block] * zs)
    inward = [inward[0]] + [swap(inward[q], "tm", 2 * q) for q in range(1, zs)]

    groups = LANES // times
    columns = part // groups
    slab = pltpu.VMEM(((rows + PAD) * columns + PAD, LANES), f32)
    flat = pltpu.VMEM((rows * columns, LANES), f32)
    scratch = [pltpu.VMEM((times, part, rows), f32), pltpu.VMEM((part * times, rows), f32), pltpu.VMEM((rows, LANES), f32)]
    scratch += [slab, slab, slab, flat, flat, slab]
    basis = time_basis(times)
    scale = np.max(np.abs(basis), 1) ** 2
    scale = np.where(scale > 1.5 / times, 2.0 / times, 1.0 / times)
    c_rows = jnp.asarray(np.tile(weights(times) * scale[None, :], (1, groups)), f32)
    work = cost(part * times * rows, 16 * SWEEPS * part * times * rows)
    *outward, keep = called(
        solve_early_kernel,
        out_shape=(shaped(2, lats, *block),) * zs + (shaped(2 * HALO * times, rows),),
        in_specs=[SMEM] + [VMEM] * 5,
        out_specs=(VMEM,) * (zs + 1),
        scratch_shapes=scratch,
        cost_estimate=work,
        compiler_params=params(24 << 20),
        name="solve_early",
    )(here, early, *coefs, c_rows)
    outward = [outward[0]] + [swap(outward[q], "tm", 2 * q) for q in range(1, zs)]
    out = called(
        solve_late_kernel,
        out_shape=shaped(times * lats, *block),
        in_specs=[SMEM] + [VMEM] * (zs + 5),
        out_specs=VMEM,
        scratch_shapes=scratch,
        cost_estimate=work,
        compiler_params=params(24 << 20),
        name="solve_late",
    )(here, *inward, keep, *coefs, c_rows)
    back = lax.all_to_all(out, ("tm", "lat"), 0, 0, tiled=True)

    plan = [(0, (q, r), q, (1, r)) for r in range(lats) for q in range(zs)]
    other = shuffle(plan, outward, [(zs, lats) + block])[0]
    other = swap(other, "tm", 1)
    plan = [(r, q, q, (0, r)) for r in range(lats) for q in range(zs)]
    plan += [(r, zs + q, zs, (q, r)) for r in range(lats) for q in range(zs)]
    home = shuffle(plan, outward + [other], [(times,) + block] * lats)
    home = [home[0]] + [swap(home[r], "lat", r) for r in range(1, lats)]
    result = pl.pallas_call(
        unpack_early_kernel,
        out_shape=shaped(fields, rl, nlon),
        in_specs=[SMEM] + [VMEM] * lats,
        out_specs=HBM,
        scratch_shapes=[dma((times * lats,))],
        cost_estimate=cost(states.size // 2),
        compiler_params=fast,
        name="unpack_early",
    )(here, *home)
    result = pl.pallas_call(
        unpack_late_kernel,
        out_shape=shaped(fields, rl, nlon),
        in_specs=[VMEM, HBM],
        out_specs=HBM,
        scratch_shapes=[dma((times * lats,))],
        input_output_aliases={1: 0},
        cost_estimate=cost(states.size // 2),
        compiler_params=fast,
        name="unpack_late",
    )(back, result)
    return result.reshape(states.shape)


def solve_general(states, mass_term, lat_coupling, lon_coupling):
    fields, tl, rl, nlon = states.shape
    tm, lats = lax.axis_size("tm"), lax.axis_size("lat")
    times, rows, parts = tl * tm, rl * lats, lats // fields
    width = nlon // (tm * parts)
    full = width + 2 * HALO
    length = padded_length(full)
    f32 = jnp.float32

    def wrapped(a):
        return jnp.concatenate([a[..., nlon - HALO :], a, a[..., :HALO]], -1)

    wide = wrapped(states)
    bands = jnp.stack([wide[..., n * width : n * width + full] for n in range(tm * parts)])
    bands = bands.reshape(tm, parts, fields, tl, rl, full).transpose(0, 2, 1, 3, 4, 5)
    got = lax.all_to_all(bands.reshape(tm * lats, tl, rl, full), ("tm", "lat"), 0, 0, tiled=True)
    field = got.reshape(tm, lats, tl, rl, full).transpose(4, 0, 2, 1, 3).reshape(full, times, rows)
    basis = jnp.asarray(time_basis(times), f32)
    b = jnp.einsum("kt,jtr->jkr", basis, field, precision=lax.Precision.HIGHEST)
    coef = wrapped(jnp.stack([mass_term, lat_coupling, lon_coupling]))
    first = lax.axis_index("tm") * parts
    mine = jnp.stack([lax.dynamic_slice_in_dim(coef, (first + n) * width, full, 2) for n in range(parts)])
    mine = jnp.broadcast_to(mine[None], (fields,) + mine.shape).reshape(lats, 3, rl, full)
    all_rows = lax.all_to_all(mine, "lat", 0, 0, tiled=True)
    m, y, x = all_rows.transpose(1, 3, 0, 2).reshape(3, full, rows)
    scale = 2.0 / DELTA
    south = jnp.concatenate([jnp.zeros((full, 1), f32), y[:, :-1]], 1)
    diag = scale * (CENTER - m - (y + south) - (x + jnp.roll(x, 1, 0)))
    lat = scale * jnp.concatenate([y[:, :-1], jnp.zeros((full, 1), f32)], 1)
    ends = ((PAD, length - PAD - full), (0, 0))
    diag, lon, lat = (jnp.pad(a, ends) for a in (diag, scale * x, lat))
    b = jnp.pad(b, (ends[0], (0, 0), (0, 0))).reshape(length * times, rows)
    c = weights(times)
    c_rows = jnp.broadcast_to(jnp.asarray(c.reshape(-1, 1), f32), ((SWEEPS + 1) * times, rows))
    slab = pltpu.VMEM((length * times, rows), f32)
    solved = pl.pallas_call(
        lambda *refs: sweep_kernel(full, *refs),
        out_shape=jax.ShapeDtypeStruct((length * times, rows), f32),
        in_specs=[VMEM] * 5,
        out_specs=VMEM,
        scratch_shapes=[slab],
        name="sweeps",
    )(b, diag, lon, lat, c_rows)
    solved = solved.reshape(length, times, rows)[PAD + HALO : PAD + HALO + width]
    field = jnp.einsum("kt,jkr->jtr", basis, solved, precision=lax.Precision.HIGHEST)
    field = field.reshape(width, tm, tl, lats, rl).transpose(1, 3, 2, 4, 0).reshape(tm * lats, tl, rl, width)
    back = lax.all_to_all(field, ("tm", "lat"), 0, 0, tiled=True)
    back = back.reshape(tm, fields, parts, tl, rl, width).transpose(1, 3, 4, 0, 2, 5)
    return back.reshape(fields, tl, rl, nlon)


def per_device(states, mass_term, lat_coupling, lon_coupling):
    fields, tl, rl, nlon = states.shape
    tm, lats = lax.axis_size("tm"), lax.axis_size("lat")
    packed = tl == 1 and tm == SUB and lats == fields == 4 and rl * lats == LANES
    packed = packed and nlon == 2 * tm * LANES and 2 * HALO * rl == SUB * LANES
    plan = solve_packed if packed else solve_general
    return plan(states, mass_term, lat_coupling, lon_coupling)


def solution(mesh):
    placed = (P(None, "tm", "lat", None), P("lat", None), P("lat", None), P("lat", None))
    return jax.shard_map(
        per_device,
        mesh=mesh,
        in_specs=placed,
        out_specs=P(None, "tm", "lat", None),
        check_vma=False,
    )
```
